256 devices in a mesh: pipe: 8 (over x, y_lo), seq: 32 (over z, y_hi, core).
Axes of the slice: x: 4, y: 4 (y_hi: 2, y_lo: 2; y = y_hi * 2 + y_lo), z: 8, core: 2. Of those that a mesh axis runs over, the one named last changes fastest.
Arguments:
- latents: bfloat16 [2, 256, 1536], P(None, 'seq', 'pipe'), may hold values from -6 to 6
- timesteps: int32 [2, 2], replicated, may hold values from 0 to 15
- step_sizes: float32 [16], replicated, may hold values from 0.2 to 0.8
- mod_table: float32 [8, 16, 4608], P('pipe'), may hold values from -4 to 4
- qk_gain: float32 [8, 2, 128], P('pipe'), may hold values from 0.5 to 2
- w_query: bfloat16 [8, 1536, 1536], P('pipe'), may hold values from -0.15625 to 0.15625
- w_kv: bfloat16 [8, 1536, 3072], P('pipe', 'seq'), may hold values from -0.15625 to 0.15625
- w_out: bfloat16 [8, 1536, 1536], P('pipe'), may hold values from -0.15625 to 0.15625
Outputs:
- final_latents: bfloat16 [2, 256, 1536], P(None, 'seq', 'pipe')
The draws below stay inside these ranges and needn't reach their ends.
All inputs are finite; a program needn't handle non-finite values.
Results may differ from the reference program's by a relative error of at most 0.025.
Values may be sent and summed in bfloat16 or wider, within the bound.
No kernel may reach another device: no remote copies, remote signals or barrier semaphores. Data moves between devices by JAX's collectives and lax.ppermute only.
A program may use at most 64 MiB of HBM per device.

```python
import math
import jax
import jax.numpy as jnp
from jax import lax

D = 1536
HEADS = 12
HEAD_DIM = 128
MICRO = 2
STEPS = 2
NT = 16
INNER = 1536
SEQ_LEN = 256
SECTIONS = 8
N_PIPE = 8


def set_ends(values, own_key, least, top_value):
    index_at = [jax.random.randint(jax.random.fold_in(own_key, axis), (), 0, length) for axis, length in enumerate(values.shape)]
    longest = values.shape.index(max(values.shape))
    beside = index_at[:longest] + [(index_at[longest] + 1) % values.shape[longest]] + index_at[longest + 1:]
    return values.at[tuple(index_at)].set(least).at[tuple(beside)].set(top_value)


def steps_of(key, shape, split, least, high):
    factor_of = 1.0
    for axis_at, blocks in split:
        draws = jax.random.uniform(jax.random.fold_in(jax.random.fold_in(key, 6), axis_at), (blocks,), jnp.float32, least / len(split), high / len(split))
        factor_of = factor_of * jnp.repeat(jnp.exp(draws), shape[axis_at] // blocks).reshape((-1,) + (1,) * (len(shape) - 1 - axis_at))
    return factor_of


def centred(rng, dims, scale, bound, shards=(), kind=jnp.bfloat16):
    drawn = jax.random.normal(rng, dims, jnp.float32) * scale
    if len(shards) > 0:
        drawn = steps_of(rng, dims, shards, -0.22, 0.18) * drawn
    return jnp.clip(drawn, min=-bound, max=bound).astype(kind)


def setup_inputs(seed: int = 0) -> dict:
    arg_keys = jax.random.split(jax.random.key(seed), 9)
    return {
        "latents": centred(arg_keys[0], (MICRO, SEQ_LEN, D), 1.0, 6.0, ((1, 32), (2, 8))),
        "timesteps": set_ends(jax.random.randint(arg_keys[1], (STEPS, MICRO), 0, NT), jax.random.fold_in(arg_keys[1], 1), 0, NT - 1).astype(jnp.int32),
        "step_sizes": jnp.clip(jnp.exp(jax.random.uniform(arg_keys[2], (NT,), jnp.float32, math.log(0.2), math.log(0.8))), 0.2, 0.8),
        "mod_table": centred(arg_keys[3], (SECTIONS, NT, 3 * D), 0.5, 4.0, ((0, 8),), jnp.float32),
        "qk_gain": jnp.clip(0.5 + 1.5 * jax.random.uniform(arg_keys[4], (SECTIONS, 2, HEAD_DIM), jnp.float32) ** steps_of(arg_keys[4], (SECTIONS, 2, HEAD_DIM), ((0, 8),), -0.2, 0.2), 0.5, 2.0),
        "w_query": centred(arg_keys[5], (SECTIONS, D, INNER), D ** -0.5, 0.15625, ((0, 8),)),
        "w_kv": centred(arg_keys[6], (SECTIONS, D, 2 * INNER), D ** -0.5, 0.15625, ((0, 8), (1, 32))),
        "w_out": centred(arg_keys[7], (SECTIONS, INNER, D), INNER ** -0.5, 0.15625, ((0, 8),)),
    }


norm_eps = 1e-06

def rms_heads(values, gain_row):
    mean_square = lax.optimization_barrier(jnp.mean(values * values, axis=-1, keepdims=True))
    return values * lax.rsqrt(mean_square + norm_eps) * gain_row

def apply_layer(hidden, mod_row, gain_pair, query_weight, kv_weight, out_weight):
    as_float = hidden.astype(jnp.float32)
    shift_row = mod_row[:D]
    scale_row = mod_row[D:2 * D]
    gate_row = mod_row[2 * D:]
    center = lax.optimization_barrier(jnp.mean(as_float, axis=-1, keepdims=True))
    spread = lax.optimization_barrier(jnp.mean(jnp.square(as_float - center), axis=-1, keepdims=True))
    modded = ((as_float - center) * lax.rsqrt(spread + norm_eps) * (1.0 + scale_row) + shift_row).astype(jnp.bfloat16)
    query_proj = jnp.dot(modded, query_weight, preferred_element_type=jnp.float32).reshape(-1, HEADS, HEAD_DIM)
    kv_proj = jnp.dot(modded, kv_weight, preferred_element_type=jnp.float32).reshape(-1, 2, HEADS, HEAD_DIM)
    queries = rms_heads(query_proj, gain_pair[0]).astype(jnp.bfloat16)
    key_rows = rms_heads(kv_proj[:, 0], gain_pair[1]).astype(jnp.bfloat16)
    value_rows = kv_proj[:, 1].astype(jnp.bfloat16)
    logits = jnp.einsum('qhd,khd->hqk', queries.astype(jnp.float32), key_rows.astype(jnp.float32)) * (1.0 / math.sqrt(HEAD_DIM))
    weights_soft = jnp.exp(logits)
    running_sum = lax.optimization_barrier(jnp.sum(weights_soft, axis=-1))
    rounded = lax.optimization_barrier(weights_soft.astype(jnp.bfloat16))
    attended = jnp.einsum('hqk,khd->hqd', rounded.astype(jnp.float32), value_rows.astype(jnp.float32)) / running_sum[..., None]
    attended = jnp.transpose(attended.astype(jnp.bfloat16), (1, 0, 2)).reshape(-1, HEADS * HEAD_DIM)
    projected_out = jnp.dot(attended, out_weight, preferred_element_type=jnp.float32)
    return (as_float + gate_row * projected_out).astype(jnp.bfloat16)

def reference(latents, timesteps, step_sizes, mod_table, qk_gain, w_query, w_kv, w_out):
    slots = [latents[slot_now] for slot_now in range(MICRO)]
    for step_now in range(STEPS):
        renewed = []
        for slot_now in range(MICRO):
            time_index = timesteps[step_now, slot_now]
            hidden = slots[slot_now]
            for segment_now in range(N_PIPE):
                hidden = apply_layer(hidden, mod_table[segment_now, time_index], qk_gain[segment_now], w_query[segment_now], w_kv[segment_now], w_out[segment_now])
            update = slots[slot_now].astype(jnp.float32) - step_sizes[time_index] * hidden.astype(jnp.float32)
            renewed.append(update.astype(jnp.bfloat16))
        slots = renewed
    return jnp.stack(slots)
```

```python
import math

import jax
import jax.numpy as jnp
from jax import lax
from jax.experimental import pallas as pl
from jax.experimental.pallas import tpu as pltpu
from jax.sharding import PartitionSpec as P

norm_eps = 1e-06


def layer_front(head_dim):
    score_scale = 1.0 / math.sqrt(head_dim)

    def body(core_ref, own_ref, other_ref, mod_ref, gain_ref, wq_ref, wkv_ref, out_ref):
        core = core_ref[0]
        half = own_ref.shape[1]
        width = 2 * half
        near = pl.multiple_of(core * half, half)
        far = pl.multiple_of((1 - core) * half, half)
        own = own_ref[...].astype(jnp.float32)
        other = other_ref[...].astype(jnp.float32)
        center = (
            jnp.sum(own, axis=-1, keepdims=True) + jnp.sum(other, axis=-1, keepdims=True)
        ) / width
        own = own - center
        other = other - center
        spread = (
            jnp.sum(own * own, axis=-1, keepdims=True)
            + jnp.sum(other * other, axis=-1, keepdims=True)
        ) / width
        inverse = lax.rsqrt(spread + norm_eps)

        def modulated(values, at):
            shift_row = mod_ref[pl.ds(at, 1), :]
            scale_row = mod_ref[pl.ds(2 + at, 1), :]
            return (values * inverse * (1.0 + scale_row) + shift_row).astype(jnp.bfloat16)

        own = modulated(own, core)
        other = modulated(other, 1 - core)

        def project(weight_ref, start, size):
            cols = pl.ds(start, size)
            return jnp.dot(
                own, weight_ref[pl.ds(near, half), cols], preferred_element_type=jnp.float32
            ) + jnp.dot(
                other, weight_ref[pl.ds(far, half), cols], preferred_element_type=jnp.float32
            )

        def rms(values, gain_row):
            mean_square = jnp.mean(values * values, axis=-1, keepdims=True)
            return (values * lax.rsqrt(mean_square + norm_eps) * gain_row).astype(jnp.bfloat16)

        gain_query = gain_ref[0:1, :]
        gain_key = gain_ref[1:2, :]
        group = 2 * head_dim
        for start in range(0, half, group):
            queries = project(wq_ref, start, group)
            keys = project(wkv_ref, start, group)
            values = project(wkv_ref, half + start, group).astype(jnp.bfloat16)
            for at in range(0, group, head_dim):
                query_head = rms(queries[:, at : at + head_dim], gain_query)
                key_head = rms(keys[:, at : at + head_dim], gain_key)
                logits = (
                    lax.dot_general(
                        query_head,
                        key_head,
                        (((1,), (1,)), ((), ())),
                        preferred_element_type=jnp.float32,
                    )
                    * score_scale
                )
                weights = jnp.exp(logits)
                total = jnp.sum(weights, axis=-1, keepdims=True)
                mixed = jnp.dot(
                    weights.astype(jnp.bfloat16),
                    values[:, at : at + head_dim],
                    preferred_element_type=jnp.float32,
                )
                out_ref[:, start + at : start + at + head_dim] = (mixed / total).astype(
                    jnp.bfloat16
                )

    return body


def layer_back(core_ref, own_ref, other_ref, hidden_ref, mod_ref, wo_ref, out_ref):
    core = core_ref[0]
    half = own_ref.shape[1]
    near = pl.multiple_of(core * half, half)
    far = pl.multiple_of((1 - core) * half, half)
    projected = jnp.dot(
        own_ref[...], wo_ref[pl.ds(near, half), :], preferred_element_type=jnp.float32
    ) + jnp.dot(other_ref[...], wo_ref[pl.ds(far, half), :], preferred_element_type=jnp.float32)
    gate_row = mod_ref[pl.ds(4 + core, 1), :]
    out_ref[...] = (hidden_ref[...].astype(jnp.float32) + gate_row * projected).astype(jnp.bfloat16)


def shards(latents, timesteps, step_sizes, mod_table, qk_gain, w_query, w_kv, w_out):
    n_pipe = lax.axis_size("pipe")
    n_seq = lax.axis_size("seq")
    pipe_at = lax.axis_index("pipe")
    seq_at = lax.axis_index("seq")
    core = seq_at % 2
    micro = (seq_at // 2) % 2
    micro_count, row_share, feature_share = latents.shape
    step_count = timesteps.shape[0]
    tokens = row_share * n_seq
    width = feature_share * n_pipe
    half = width // 2
    head_dim = qk_gain.shape[2]
    core_pairs = [(at, at ^ 1) for at in range(n_seq)]
    quads = [[4 * at + j for j in range(4)] for at in range(n_seq // 4)]

    def swapped(value):
        return lax.ppermute(value, "seq", core_pairs)

    def columns(value, side, axis):
        return lax.dynamic_slice_in_dim(value, side * half, half, axis)

    pair = w_kv[0].reshape(w_kv.shape[1], 2, half * 2)
    mine = columns(pair, core, 2)
    theirs = swapped(columns(pair, 1 - core, 2))
    mine = mine.reshape(mine.shape[0], width)
    theirs = theirs.reshape(mine.shape)
    low = jnp.where(core == 0, mine, theirs)
    high = jnp.where(core == 0, theirs, mine)
    block = jnp.concatenate([low, high], axis=0)
    theirs = lax.ppermute(block, "seq", [(at, at ^ 2) for at in range(n_seq)])
    low = jnp.where(micro == 0, block, theirs)
    high = jnp.where(micro == 0, theirs, block)
    block = jnp.concatenate([low, high], axis=0)
    block_rows = block.shape[0]
    ring = n_seq // 4
    place = seq_at // 4
    rings = [[(at, (at + turn) % n_seq) for at in range(n_seq)] for turn in (4, -4)]
    kv_half = jnp.zeros((ring * block_rows, width), jnp.bfloat16)

    def placed(whole, part, at):
        return lax.dynamic_update_slice_in_dim(whole, part, ((place + at) % ring) * block_rows, 0)

    kv_half = placed(kv_half, block, 0)
    rising = falling = block
    for turn in range(1, ring // 2 + 1):
        rising = lax.ppermute(rising, "seq", rings[0])
        kv_half = placed(kv_half, rising, ring - turn)
        if turn < ring - turn:
            falling = lax.ppermute(falling, "seq", rings[1])
            kv_half = placed(kv_half, falling, turn)
    query_half = columns(w_query[0], core, 1)
    out_half = columns(w_out[0], core, 1)
    core_word = core.astype(jnp.int32).reshape(1)

    taus = lax.dynamic_index_in_dim(timesteps, micro, 1, keepdims=False)
    mods = [
        lax.dynamic_index_in_dim(mod_table[0], taus[at], 0, keepdims=False).reshape(6, half)
        for at in range(step_count)
    ]
    first_size = lax.dynamic_index_in_dim(step_sizes, taus[0], 0, keepdims=False)
    last_sizes = jnp.stack([step_sizes[timesteps[step_count - 1, at]] for at in range(micro_count)])

    sent = jnp.broadcast_to(latents[None], (n_pipe,) + latents.shape)
    rows = lax.all_to_all(sent, "pipe", 0, 0, tiled=True)
    rows = jnp.transpose(rows, (1, 2, 0, 3)).reshape(micro_count, row_share, 2, half)
    sent = jnp.transpose(rows, (0, 2, 1, 3)).reshape(1, 4, row_share, half)
    sent = jnp.broadcast_to(sent, (n_seq // 4, 4, row_share, half)).reshape(
        n_seq, row_share, half
    )
    slot = lax.all_to_all(sent, "seq", 0, 0, tiled=True).reshape(tokens, half)

    smem = pl.BlockSpec(memory_space=pltpu.SMEM)
    vmem = pl.BlockSpec(memory_space=pltpu.VMEM)
    front = pl.pallas_call(
        layer_front(head_dim),
        out_shape=jax.ShapeDtypeStruct((tokens, half), jnp.bfloat16),
        in_specs=[smem] + [vmem] * 6,
        out_specs=vmem,
        compiler_params=pltpu.CompilerParams(vmem_limit_bytes=32 << 20),
        name="front",
    )
    back = pl.pallas_call(
        layer_back,
        out_shape=jax.ShapeDtypeStruct((tokens, half), jnp.bfloat16),
        in_specs=[smem] + [vmem] * 5,
        out_specs=vmem,
        compiler_params=pltpu.CompilerParams(vmem_limit_bytes=16 << 20),
        name="back",
    )

    hidden = slot
    for tick in range(step_count * n_pipe):
        step = tick // n_pipe
        if tick > 0:
            hidden = lax.ppermute(hidden, "pipe", [((tick - 1) % n_pipe, tick % n_pipe)])
        if tick > 0 and tick % n_pipe == 0:
            slot = (
                slot.astype(jnp.float32) - first_size * hidden.astype(jnp.float32)
            ).astype(jnp.bfloat16)
            hidden = slot
        attended = front(
            core_word, hidden, swapped(hidden), mods[step], qk_gain[0], query_half, kv_half
        )
        hidden = back(core_word, attended, swapped(attended), hidden, mods[step], out_half)

    kept = jnp.where(pipe_at == 0, slot, hidden)
    kept = lax.dynamic_slice_in_dim(kept, (seq_at // 4) * 4 * row_share, 4 * row_share, 0)
    kept = kept.reshape(4, row_share, half)
    kept = lax.all_to_all(kept, "seq", 0, 0, tiled=True, axis_index_groups=quads)
    kept = kept.reshape(micro_count, 2, row_share, n_pipe // 2, feature_share)
    sent = jnp.transpose(kept, (1, 3, 0, 2, 4)).reshape(
        n_pipe, micro_count, row_share, feature_share
    )
    got = lax.all_to_all(sent, "pipe", 0, 0, tiled=True).astype(jnp.float32)
    return (got[0] - last_sizes[:, None, None] * got[n_pipe - 1]).astype(jnp.bfloat16)


def solution(mesh):
    in_specs = (
        P(None, "seq", "pipe"),
        P(),
        P(),
        P("pipe", None, None),
        P("pipe", None, None),
        P("pipe", None, None),
        P("pipe", "seq", None),
        P("pipe", None, None),
    )
    out_specs = P(None, "seq", "pipe")
    return jax.shard_map(shards, mesh=mesh, in_specs=in_specs, out_specs=out_specs, check_vma=False)
```

```python
import math

import jax
import jax.numpy as jnp
from jax import lax
from jax.experimental import pallas as pl
from jax.experimental.pallas import tpu as pltpu
from jax.sharding import PartitionSpec as P

norm_eps = 1e-06


def layer_front(head_dim, step):
    score_scale = 1.0 / math.sqrt(head_dim)

    def body(
        word_ref, time_ref, own_ref, other_ref, mod_ref, gain_ref, wq_ref, wkv_ref, out_ref
    ):
        core = word_ref[0]
        tau = time_ref[step, word_ref[1]]
        half = own_ref.shape[1]
        width = 2 * half
        near = pl.multiple_of(core * half, half)
        far = pl.multiple_of((1 - core) * half, half)
        own = own_ref[...].astype(jnp.float32)
        other = other_ref[...].astype(jnp.float32)
        center = (
            jnp.sum(own, axis=-1, keepdims=True) + jnp.sum(other, axis=-1, keepdims=True)
        ) / width
        own = own - center
        other = other - center
        spread = (
            jnp.sum(own * own, axis=-1, keepdims=True)
            + jnp.sum(other * other, axis=-1, keepdims=True)
        ) / width
        inverse = lax.rsqrt(spread + norm_eps)

        def modulated(values, at):
            shift_row = mod_ref[pl.ds(tau, 1), pl.ds(pl.multiple_of(at * half, half), half)]
            scale_row = mod_ref[pl.ds(tau, 1), pl.ds(pl.multiple_of((2 + at) * half, half), half)]
            return (values * inverse * (1.0 + scale_row) + shift_row).astype(jnp.bfloat16)

        own = modulated(own, core)
        other = modulated(other, 1 - core)

        def project(weight_ref, start, size):
            cols = pl.ds(start, size)
            return jnp.dot(
                own, weight_ref[pl.ds(near, half), cols], preferred_element_type=jnp.float32
            ) + jnp.dot(
                other, weight_ref[pl.ds(far, half), cols], preferred_element_type=jnp.float32
            )

        def rms(values, gain_row):
            mean_square = jnp.mean(values * values, axis=-1, keepdims=True)
            return (values * lax.rsqrt(mean_square + norm_eps) * gain_row).astype(jnp.bfloat16)

        gain_query = gain_ref[0:1, :]
        gain_key = gain_ref[1:2, :]
        group = 2 * head_dim
        for start in range(0, half, group):
            queries = project(wq_ref, start, group)
            keys = project(wkv_ref, start, group)
            values = project(wkv_ref, half + start, group).astype(jnp.bfloat16)
            for at in range(0, group, head_dim):
                query_head = rms(queries[:, at : at + head_dim], gain_query)
                key_head = rms(keys[:, at : at + head_dim], gain_key)
                logits = (
                    lax.dot_general(
                        query_head,
                        key_head,
                        (((1,), (1,)), ((), ())),
                        preferred_element_type=jnp.float32,
                    )
                    * score_scale
                )
                weights = jnp.exp(logits)
                total = jnp.sum(weights, axis=-1, keepdims=True)
                mixed = jnp.dot(
                    weights.astype(jnp.bfloat16),
                    values[:, at : at + head_dim],
                    preferred_element_type=jnp.float32,
                )
                out_ref[:, start + at : start + at + head_dim] = (mixed / total).astype(
                    jnp.bfloat16
                )

    return body


def layer_back(step):
    def body(word_ref, time_ref, own_ref, other_ref, hidden_ref, mod_ref, wo_ref, out_ref):
        core = word_ref[0]
        tau = time_ref[step, word_ref[1]]
        half = own_ref.shape[1]
        near = pl.multiple_of(core * half, half)
        far = pl.multiple_of((1 - core) * half, half)
        projected = jnp.dot(
            own_ref[...], wo_ref[pl.ds(near, half), :], preferred_element_type=jnp.float32
        ) + jnp.dot(
            other_ref[...], wo_ref[pl.ds(far, half), :], preferred_element_type=jnp.float32
        )
        gate_row = mod_ref[pl.ds(tau, 1), pl.ds(pl.multiple_of((4 + core) * half, half), half)]
        out_ref[...] = (hidden_ref[...].astype(jnp.float32) + gate_row * projected).astype(
            jnp.bfloat16
        )

    return body


def load_own(spots):
    def body(word_ref, *refs):
        part_refs = refs[: len(spots)]
        query_ref, out_ref = refs[len(spots) : len(spots) + 2]
        query_held, kv_held, out_held, sems = refs[len(spots) + 2 :]
        half = query_held.shape[1]
        ring = kv_held.shape[0] // part_refs[0].shape[0]
        block = kv_held.shape[0] // ring
        copies = []
        for index, ((turn, start), part_ref) in enumerate(zip(spots, part_refs)):
            rows = part_ref.shape[0]
            at = pl.multiple_of(lax.rem(word_ref[2] + turn, ring) * block + start, rows)
            copies.append(
                pltpu.make_async_copy(part_ref, kv_held.at[pl.ds(at, rows), :], sems.at[index])
            )
        cols = pl.ds(pl.multiple_of(word_ref[0] * half, half), half)
        for index, (source, held) in enumerate(((query_ref, query_held), (out_ref, out_held))):
            copies.append(
                pltpu.make_async_copy(source.at[0, :, cols], held, sems.at[len(spots) + index])
            )
        for copy in copies:
            copy.start()
        for copy in copies:
            copy.wait()

    return body


def load_next(*refs):
    count = (len(refs) - 1) // 2
    sems = refs[-1]
    copies = [
        pltpu.make_async_copy(refs[at], refs[count + at], sems.at[at]) for at in range(count)
    ]
    for copy in copies:
        copy.start()
    for copy in copies:
        copy.wait()


def advance_slot(step):
    def body(word_ref, time_ref, size_ref, slot_ref, hidden_ref, out_ref):
        size = size_ref[time_ref[step, word_ref[1]]]
        out_ref[...] = (
            slot_ref[...].astype(jnp.float32) - size * hidden_ref[...].astype(jnp.float32)
        ).astype(jnp.bfloat16)

    return body


def shards(latents, timesteps, step_sizes, mod_table, qk_gain, w_query, w_kv, w_out):
    n_pipe = lax.axis_size("pipe")
    n_seq = lax.axis_size("seq")
    pipe_at = lax.axis_index("pipe")
    seq_at = lax.axis_index("seq")
    core = seq_at % 2
    micro = (seq_at // 2) % 2
    micro_count, row_share, feature_share = latents.shape
    step_count = timesteps.shape[0]
    tokens = row_share * n_seq
    width = feature_share * n_pipe
    half = width // 2
    head_dim = qk_gain.shape[2]
    core_pairs = [(at, at ^ 1) for at in range(n_seq)]
    quads = [[4 * at + j for j in range(4)] for at in range(n_seq // 4)]

    def swapped(value):
        return lax.ppermute(value, "seq", core_pairs)

    def columns(value, side, axis):
        return lax.dynamic_slice_in_dim(value, side * half, half, axis)

    pair = w_kv[0].reshape(w_kv.shape[1], 2, half * 2)
    mine = columns(pair, core, 2)
    theirs = swapped(columns(pair, 1 - core, 2))
    mine = mine.reshape(mine.shape[0], width)
    theirs = theirs.reshape(mine.shape)
    low = jnp.where(core == 0, mine, theirs)
    high = jnp.where(core == 0, theirs, mine)
    block = jnp.concatenate([low, high], axis=0)
    latents, block = lax.optimization_barrier((latents, block))
    theirs = lax.ppermute(block, "seq", [(at, at ^ 2) for at in range(n_seq)])

    sent = jnp.broadcast_to(latents[None], (n_pipe,) + latents.shape)
    rows = lax.all_to_all(sent, "pipe", 0, 0, tiled=True)
    low = jnp.where(micro == 0, block, theirs)
    high = jnp.where(micro == 0, theirs, block)
    block = jnp.concatenate([low, high], axis=0)
    rows, block = lax.optimization_barrier((rows, block))
    ring = n_seq // 4
    rings = [[(at, (at + turn) % n_seq) for at in range(n_seq)] for turn in (4, -4)]
    middle = block.shape[0] // 2
    rising = falling = block
    parts = [block]
    spots = [(0, 0)]
    for turn in range(1, ring // 2):
        rising = lax.ppermute(rising, "seq", rings[0])
        falling = lax.ppermute(falling, "seq", rings[1])
        parts += [rising, falling]
        spots += [(ring - turn, 0), (turn, 0)]
        if turn == 1:
            rows, rising, falling = lax.optimization_barrier((rows, rising, falling))
    parts += [
        lax.ppermute(rising[:middle], "seq", rings[0]),
        lax.ppermute(falling[middle:], "seq", rings[1]),
    ]
    spots += [(ring // 2, 0), (ring // 2, middle)]

    rows = jnp.transpose(rows, (1, 2, 0, 3)).reshape(micro_count, row_share, 2, half)
    sent = jnp.transpose(rows, (0, 2, 1, 3)).reshape(1, 4, row_share, half)
    sent = jnp.broadcast_to(sent, (n_seq // 4, 4, row_share, half)).reshape(
        n_seq, row_share, half
    )
    slot = lax.all_to_all(sent, "seq", 0, 0, tiled=True).reshape(tokens, half)

    words = jnp.stack([core, micro, seq_at // 4]).astype(jnp.int32)
    last_sizes = jnp.stack([step_sizes[timesteps[step_count - 1, at]] for at in range(micro_count)])
    smem = pl.BlockSpec(memory_space=pltpu.SMEM)
    vmem = pl.BlockSpec(memory_space=pltpu.VMEM)
    hbm = pl.BlockSpec(memory_space=pltpu.HBM)
    held_shapes = [
        jax.ShapeDtypeStruct(shape, jnp.bfloat16)
        for shape in ((width, half), (width, width), (width, half))
    ]
    held = pl.pallas_call(
        load_own(spots),
        out_shape=held_shapes,
        in_specs=[smem] + [hbm] * (len(parts) + 2),
        out_specs=[vmem] * 3,
        scratch_shapes=[pltpu.SemaphoreType.DMA((len(parts) + 2,))],
        compiler_params=pltpu.CompilerParams(vmem_limit_bytes=12 << 20),
        name="load_own",
    )(words, *parts, w_query, w_out)
    lone = (mod_table[0], qk_gain[0], *held)

    def layer(hidden, step, weights):
        mods, gains, query_part, kv_part, out_part = weights
        attended = pl.pallas_call(
            layer_front(head_dim, step),
            out_shape=jax.ShapeDtypeStruct((tokens, half), jnp.bfloat16),
            in_specs=[smem] * 2 + [vmem] * 6,
            out_specs=vmem,
            compiler_params=pltpu.CompilerParams(vmem_limit_bytes=16 << 20),
            name="front",
        )(words, timesteps, hidden, swapped(hidden), mods, gains, query_part, kv_part)
        return pl.pallas_call(
            layer_back(step),
            out_shape=jax.ShapeDtypeStruct((tokens, half), jnp.bfloat16),
            in_specs=[smem] * 2 + [vmem] * 5,
            out_specs=vmem,
            compiler_params=pltpu.CompilerParams(vmem_limit_bytes=12 << 20),
            name="back",
        )(words, timesteps, attended, swapped(attended), hidden, mods, out_part)

    holder = 0
    hidden = slot
    for step in range(step_count):
        for section in range(n_pipe):
            if section != holder:
                hidden = lax.ppermute(hidden, "pipe", [(holder, section)])
                holder = section
            if step > 0 and section == 0:
                slot = pl.pallas_call(
                    advance_slot(step - 1),
                    out_shape=jax.ShapeDtypeStruct((tokens, half), jnp.bfloat16),
                    in_specs=[smem] * 3 + [vmem] * 2,
                    out_specs=vmem,
                    compiler_params=pltpu.CompilerParams(vmem_limit_bytes=8 << 20),
                    name="advance_slot",
                )(words, timesteps, step_sizes, slot, hidden)
                hidden = slot
            hidden = layer(hidden, step, lone)

    kept = jnp.where(pipe_at == 0, slot, hidden)
    kept = lax.dynamic_slice_in_dim(kept, (seq_at // 4) * 4 * row_share, 4 * row_share, 0)
    kept = kept.reshape(4, row_share, half)
    kept = lax.all_to_all(kept, "seq", 0, 0, tiled=True, axis_index_groups=quads)
    kept = kept.reshape(micro_count, 2, row_share, n_pipe // 2, feature_share)
    sent = jnp.transpose(kept, (1, 3, 0, 2, 4)).reshape(
        n_pipe, micro_count, row_share, feature_share
    )
    got = lax.all_to_all(sent, "pipe", 0, 0, tiled=True).astype(jnp.float32)
    return (got[0] - last_sizes[:, None, None] * got[holder]).astype(jnp.bfloat16)


def solution(mesh):
    in_specs = (
        P(None, "seq", "pipe"),
        P(),
        P(),
        P("pipe", None, None),
        P("pipe", None, None),
        P("pipe", None, None),
        P("pipe", "seq", None),
        P("pipe", None, None),
    )
    out_specs = P(None, "seq", "pipe")
    return jax.shard_map(shards, mesh=mesh, in_specs=in_specs, out_specs=out_specs, check_vma=False)
```

```python
import math

import jax
import jax.numpy as jnp
from jax import lax
from jax.experimental import pallas as pl
from jax.experimental.pallas import tpu as pltpu
from jax.sharding import PartitionSpec as P

norm_eps = 1e-06


def layer_front(head_dim):
    score_scale = 1.0 / math.sqrt(head_dim)

    def body(own_ref, other_ref, mod_ref, gain_ref, wq_ref, wkv_ref, out_ref):
        half = own_ref.shape[1]
        width = 2 * half
        own = own_ref[...].astype(jnp.float32)
        other = other_ref[...].astype(jnp.float32)
        center = (
            jnp.sum(own, axis=-1, keepdims=True) + jnp.sum(other, axis=-1, keepdims=True)
        ) / width
        own = own - center
        other = other - center
        spread = (
            jnp.sum(own * own, axis=-1, keepdims=True)
            + jnp.sum(other * other, axis=-1, keepdims=True)
        ) / width
        inverse = lax.rsqrt(spread + norm_eps)

        def modulated(values, at):
            shift_row = mod_ref[at : at + 1, :]
            scale_row = mod_ref[2 + at : 3 + at, :]
            return (values * inverse * (1.0 + scale_row) + shift_row).astype(jnp.bfloat16)

        own = modulated(own, 0)
        other = modulated(other, 1)

        def project(weight_ref, start, size):
            cols = slice(start, start + size)
            return jnp.dot(
                own, weight_ref[:half, cols], preferred_element_type=jnp.float32
            ) + jnp.dot(other, weight_ref[half:, cols], preferred_element_type=jnp.float32)

        def rms(values, gain_row):
            mean_square = jnp.mean(values * values, axis=-1, keepdims=True)
            return (values * lax.rsqrt(mean_square + norm_eps) * gain_row).astype(jnp.bfloat16)

        gain_query = gain_ref[0:1, :]
        gain_key = gain_ref[1:2, :]
        group = 2 * head_dim
        for start in range(0, half, group):
            queries = project(wq_ref, start, group)
            keys = project(wkv_ref, start, group)
            values = project(wkv_ref, half + start, group).astype(jnp.bfloat16)
            for at in range(0, group, head_dim):
                query_head = rms(queries[:, at : at + head_dim], gain_query)
                key_head = rms(keys[:, at : at + head_dim], gain_key)
                logits = (
                    lax.dot_general(
                        query_head,
                        key_head,
                        (((1,), (1,)), ((), ())),
                        preferred_element_type=jnp.float32,
                    )
                    * score_scale
                )
                weights = jnp.exp(logits)
                total = jnp.sum(weights, axis=-1, keepdims=True)
                mixed = jnp.dot(
                    weights.astype(jnp.bfloat16),
                    values[:, at : at + head_dim],
                    preferred_element_type=jnp.float32,
                )
                out_ref[:, start + at : start + at + head_dim] = (mixed / total).astype(
                    jnp.bfloat16
                )

    return body


def layer_back(own_ref, other_ref, hidden_ref, mod_ref, wo_ref, out_ref):
    half = own_ref.shape[1]
    projected = jnp.dot(
        own_ref[...], wo_ref[:half, :], preferred_element_type=jnp.float32
    ) + jnp.dot(other_ref[...], wo_ref[half:, :], preferred_element_type=jnp.float32)
    out_ref[...] = (
        hidden_ref[...].astype(jnp.float32) + mod_ref[4:5, :] * projected
    ).astype(jnp.bfloat16)


def load_own(spots):
    def body(word_ref, *refs):
        part_refs = refs[: len(spots)]
        time_ref, mod_ref, gain_ref, query_ref, out_ref = refs[len(spots) : len(spots) + 5]
        query_held, kv_held, out_held, gain_held = refs[len(spots) + 5 : len(spots) + 9]
        mods_held, sems = refs[len(spots) + 9 : -1], refs[-1]
        core = word_ref[0]
        width, half = query_held.shape
        block = part_refs[0].shape[0]
        ring = width // block
        copies = []

        def copied(source, target):
            copies.append(pltpu.make_async_copy(source, target, sems.at[len(copies)]))

        for (turn, start), part_ref in zip(spots, part_refs):
            rows = part_ref.shape[0]
            at = lax.rem(word_ref[2] + turn + core * (ring // 2), ring) * block + start
            copied(part_ref, kv_held.at[pl.ds(pl.multiple_of(at, rows), rows), :])
        cols = pl.ds(pl.multiple_of(core * half, half), half)
        for source, held in ((query_ref, query_held), (out_ref, out_held)):
            for side in range(2):
                first = pl.multiple_of(lax.rem(core + side, 2) * half, half)
                copied(
                    source.at[0, pl.ds(first, half), cols], held.at[pl.ds(side * half, half), :]
                )
        for copy in copies:
            copy.start()
        gain_held[...] = gain_ref[0]
        for step, held in enumerate(mods_held):
            row = pl.ds(time_ref[step, word_ref[1]], 1)
            for third in range(3):
                for side in range(2):
                    first = (2 * third + lax.rem(core + side, 2)) * half
                    first = pl.ds(pl.multiple_of(first, half), half)
                    held[2 * third + side : 2 * third + side + 1, :] = mod_ref[0, row, first]
        for copy in copies:
            copy.wait()

    return body


def advance_slot(step):
    def body(word_ref, time_ref, size_ref, slot_ref, hidden_ref, out_ref):
        size = size_ref[time_ref[step, word_ref[1]]]
        out_ref[...] = (
            slot_ref[...].astype(jnp.float32) - size * hidden_ref[...].astype(jnp.float32)
        ).astype(jnp.bfloat16)

    return body


def finish(step, holder):
    def body(time_ref, size_ref, got_ref, out_ref):
        for micro in range(out_ref.shape[0]):
            size = size_ref[time_ref[step, micro]]
            slot = got_ref[0, micro].astype(jnp.float32)
            hidden = got_ref[holder, micro].astype(jnp.float32)
            out_ref[micro] = (slot - size * hidden).astype(jnp.bfloat16)

    return body


def shards(latents, timesteps, step_sizes, mod_table, qk_gain, w_query, w_kv, w_out):
    n_pipe = lax.axis_size("pipe")
    n_seq = lax.axis_size("seq")
    pipe_at = lax.axis_index("pipe")
    seq_at = lax.axis_index("seq")
    core = seq_at % 2
    micro = (seq_at // 2) % 2
    micro_count, row_share, feature_share = latents.shape
    step_count = timesteps.shape[0]
    tokens = row_share * n_seq
    width = feature_share * n_pipe
    half = width // 2
    head_dim = qk_gain.shape[2]
    core_pairs = [(at, at ^ 1) for at in range(n_seq)]
    quads = [[4 * at + j for j in range(4)] for at in range(n_seq // 4)]

    def swapped(value):
        return lax.ppermute(value, "seq", core_pairs)

    def columns(value, side, axis):
        return lax.dynamic_slice_in_dim(value, side * half, half, axis)

    def kv_columns(side):
        keys, values = w_kv[0, :, :width], w_kv[0, :, width:]
        return jnp.concatenate([columns(keys, side, 1), columns(values, side, 1)], axis=1)

    mine = kv_columns(core)
    theirs = swapped(kv_columns(1 - core))
    low = jnp.where(core == 0, mine, theirs)
    high = jnp.where(core == 0, theirs, mine)
    block = jnp.concatenate([low, high], axis=0)
    latents, block = lax.optimization_barrier((latents, block))
    theirs = lax.ppermute(block, "seq", [(at, at ^ 2) for at in range(n_seq)])

    sent = jnp.broadcast_to(latents[None], (n_pipe,) + latents.shape)
    rows = lax.all_to_all(sent, "pipe", 0, 0, tiled=True)
    low = jnp.where(micro == 0, block, theirs)
    high = jnp.where(micro == 0, theirs, block)
    block = jnp.concatenate([low, high], axis=0)
    backward = [(at + 1, at) for at in range(0, n_pipe, 2)]

    def to_even(value):
        return lax.ppermute(value, "pipe", backward)

    rows, block = lax.optimization_barrier((rows, block))
    ring = n_seq // 4
    rings = [[(at, (at + turn) % n_seq) for at in range(n_seq)] for turn in (4, -4)]
    middle = block.shape[0] // 2
    rising = falling = block
    parts = [block]
    spots = [(0, 0)]
    for turn in range(1, ring // 2):
        rising = lax.ppermute(rising, "seq", rings[0])
        falling = lax.ppermute(falling, "seq", rings[1])
        parts += [rising, falling]
        spots += [(ring - turn, 0), (turn, 0)]
        if turn == 1:
            rows, rising, falling = lax.optimization_barrier((rows, rising, falling))
    parts += [
        lax.ppermute(rising[:middle], "seq", rings[0]),
        lax.ppermute(falling[middle:], "seq", rings[1]),
    ]
    spots += [(ring // 2, 0), (ring // 2, middle)]

    rows = jnp.transpose(rows, (1, 2, 0, 3)).reshape(micro_count, row_share, 2, half)
    sent = jnp.transpose(rows, (0, 2, 1, 3)).reshape(1, 4, row_share, half)
    sent = jnp.broadcast_to(sent, (n_seq // 4, 4, row_share, half)).reshape(
        n_seq, row_share, half
    )
    slot = lax.all_to_all(sent, "seq", 0, 0, tiled=True).reshape(tokens, half)

    words = jnp.stack([core, micro, seq_at // 4]).astype(jnp.int32)
    smem = pl.BlockSpec(memory_space=pltpu.SMEM)
    vmem = pl.BlockSpec(memory_space=pltpu.VMEM)
    hbm = pl.BlockSpec(memory_space=pltpu.HBM)
    held_shapes = [
        jax.ShapeDtypeStruct(shape, jnp.bfloat16)
        for shape in ((width, half), (width, width), (width, half))
    ]
    small_shapes = [jax.ShapeDtypeStruct(qk_gain.shape[1:], jnp.float32)] + [
        jax.ShapeDtypeStruct((6, half), jnp.float32)
    ] * step_count

    def in_hbm(value):
        return pltpu.with_memory_space_constraint(value, pltpu.HBM)

    loaded = pl.pallas_call(
        load_own(spots),
        out_shape=held_shapes + small_shapes,
        in_specs=[smem] + [hbm] * len(parts) + [smem, vmem, vmem, hbm, hbm],
        out_specs=[vmem] * (4 + step_count),
        scratch_shapes=[pltpu.SemaphoreType.DMA((len(parts) + 4,))],
        compiler_params=pltpu.CompilerParams(vmem_limit_bytes=12 << 20),
        name="load_own",
    )(
        words,
        *(in_hbm(part) for part in parts),
        timesteps,
        mod_table,
        qk_gain,
        in_hbm(w_query),
        in_hbm(w_out),
    )
    held, gains, mods = loaded[:3], loaded[3], loaded[4:]

    def layer(hidden, mods, gains, query_part, kv_part, out_part):
        attended = pl.pallas_call(
            layer_front(head_dim),
            out_shape=jax.ShapeDtypeStruct((tokens, half), jnp.bfloat16),
            in_specs=[vmem] * 6,
            out_specs=vmem,
            compiler_params=pltpu.CompilerParams(vmem_limit_bytes=16 << 20),
            name="front",
        )(hidden, swapped(hidden), mods, gains, query_part, kv_part)
        return pl.pallas_call(
            layer_back,
            out_shape=jax.ShapeDtypeStruct((tokens, half), jnp.bfloat16),
            in_specs=[vmem] * 5,
            out_specs=vmem,
            compiler_params=pltpu.CompilerParams(vmem_limit_bytes=12 << 20),
            name="back",
        )(attended, swapped(attended), hidden, mods, out_part)

    following = [to_even(value) for value in (mods[-1], gains, *held)]
    due = {2: (2,), 4: (0, 1, 4), n_pipe: (3,)}

    holder = 0
    hidden = slot
    for step in range(step_count):
        for section in range(n_pipe):
            joined = step > 0
            place = section - section % 2 if joined else section
            if place != holder:
                hidden = lax.ppermute(hidden, "pipe", [(holder, place)])
                holder = place
            if step > 0 and section == 0:
                slot = pl.pallas_call(
                    advance_slot(step - 1),
                    out_shape=jax.ShapeDtypeStruct((tokens, half), jnp.bfloat16),
                    in_specs=[smem] * 3 + [vmem] * 2,
                    out_specs=vmem,
                    compiler_params=pltpu.CompilerParams(vmem_limit_bytes=8 << 20),
                    name="advance_slot",
                )(words, timesteps, step_sizes, slot, hidden)
                hidden = slot
            hidden = layer(hidden, *(following if section != place else (mods[step], gains, *held)))
            for at in due.get(step * n_pipe + section, ()):
                hidden, following[at] = lax.optimization_barrier((hidden, following[at]))

    kept = jnp.where(pipe_at == 0, slot, hidden)
    kept = lax.dynamic_slice_in_dim(kept, (seq_at // 4) * 4 * row_share, 4 * row_share, 0)
    kept = kept.reshape(4, row_share, half)
    kept = lax.all_to_all(kept, "seq", 0, 0, tiled=True, axis_index_groups=quads)
    kept = kept.reshape(micro_count, 2, row_share, n_pipe // 2, feature_share)
    sent = jnp.transpose(kept, (1, 3, 0, 2, 4)).reshape(
        n_pipe, micro_count, row_share, feature_share
    )
    got = lax.all_to_all(sent, "pipe", 0, 0, tiled=True)
    return pl.pallas_call(
        finish(step_count - 1, holder),
        out_shape=jax.ShapeDtypeStruct(latents.shape, jnp.bfloat16),
        in_specs=[smem] * 2 + [vmem],
        out_specs=vmem,
        compiler_params=pltpu.CompilerParams(vmem_limit_bytes=8 << 20),
        name="finish",
    )(timesteps, step_sizes, got)


def solution(mesh):
    in_specs = (
        P(None, "seq", "pipe"),
        P(),
        P(),
        P("pipe", None, None),
        P("pipe", None, None),
        P("pipe", None, None),
        P("pipe", "seq", None),
        P("pipe", None, None),
    )
    out_specs = P(None, "seq", "pipe")
    return jax.shard_map(shards, mesh=mesh, in_specs=in_specs, out_specs=out_specs, check_vma=False)
```

```python
import math

import jax
import jax.numpy as jnp
from jax import lax
from jax.experimental import pallas as pl
from jax.experimental.pallas import tpu as pltpu
from jax.sharding import PartitionSpec as P

norm_eps = 1e-06


def layer_front(head_dim):
    score_scale = 1.0 / math.sqrt(head_dim)

    def body(own_ref, other_ref, mod_ref, gain_ref, weight_ref, out_ref):
        half = own_ref.shape[1]
        width = 2 * half
        own = own_ref[...].astype(jnp.float32)
        other = other_ref[...].astype(jnp.float32)
        center = (
            jnp.sum(own, axis=-1, keepdims=True) + jnp.sum(other, axis=-1, keepdims=True)
        ) / width
        own = own - center
        other = other - center
        spread = (
            jnp.sum(own * own, axis=-1, keepdims=True)
            + jnp.sum(other * other, axis=-1, keepdims=True)
        ) / width
        inverse = lax.rsqrt(spread + norm_eps)

        def modulated(values, at):
            shift_row = mod_ref[at : at + 1, :]
            scale_row = mod_ref[2 + at : 3 + at, :]
            return (values * inverse * (1.0 + scale_row) + shift_row).astype(jnp.bfloat16)

        own = modulated(own, 0)
        other = modulated(other, 1)

        def project(start, size):
            cols = slice(start, start + size)
            return jnp.dot(
                own, weight_ref[:half, cols], preferred_element_type=jnp.float32
            ) + jnp.dot(other, weight_ref[half:, cols], preferred_element_type=jnp.float32)

        def rms(values, gain_row):
            mean_square = jnp.mean(values * values, axis=-1, keepdims=True)
            return (values * lax.rsqrt(mean_square + norm_eps) * gain_row).astype(jnp.bfloat16)

        gain_query = gain_ref[0:1, :]
        gain_key = gain_ref[1:2, :]
        group = 2 * head_dim
        for start in range(0, half, group):
            queries = project(start, group)
            keys = project(half + start, group)
            values = project(2 * half + start, group).astype(jnp.bfloat16)
            for at in range(0, group, head_dim):
                query_head = rms(queries[:, at : at + head_dim], gain_query)
                key_head = rms(keys[:, at : at + head_dim], gain_key)
                logits = (
                    lax.dot_general(
                        query_head,
                        key_head,
                        (((1,), (1,)), ((), ())),
                        preferred_element_type=jnp.float32,
                    )
                    * score_scale
                )
                weights = jnp.exp(logits)
                total = jnp.sum(weights, axis=-1, keepdims=True)
                mixed = jnp.dot(
                    weights.astype(jnp.bfloat16),
                    values[:, at : at + head_dim],
                    preferred_element_type=jnp.float32,
                )
                out_ref[:, start + at : start + at + head_dim] = (mixed / total).astype(
                    jnp.bfloat16
                )

    return body


def layer_back(own_ref, other_ref, hidden_ref, mod_ref, weight_ref, out_ref):
    half = own_ref.shape[1]
    cols = slice(3 * half, 4 * half)
    projected = jnp.dot(
        own_ref[...], weight_ref[:half, cols], preferred_element_type=jnp.float32
    ) + jnp.dot(other_ref[...], weight_ref[half:, cols], preferred_element_type=jnp.float32)
    out_ref[...] = (
        hidden_ref[...].astype(jnp.float32) + mod_ref[4:5, :] * projected
    ).astype(jnp.bfloat16)


def load_own(spots):
    def body(word_ref, *refs):
        part_refs = refs[: len(spots)]
        time_ref, mod_ref, gain_ref, next_mod_ref, next_gain_ref, query_ref, out_ref = refs[
            len(spots) : len(spots) + 7
        ]
        held_ref, gain_held, next_gain_held, next_mods_held = refs[
            len(spots) + 7 : len(spots) + 11
        ]
        mods_held, sems = refs[len(spots) + 11 : -1], refs[-1]
        core = word_ref[0]
        width = held_ref.shape[0]
        half = width // 2
        block = part_refs[0].shape[0]
        ring = width // block
        copies = []

        def copied(source, target):
            copies.append(pltpu.make_async_copy(source, target, sems.at[len(copies)]))

        for (turn, start), part_ref in zip(spots, part_refs):
            rows = part_ref.shape[0]
            at = lax.rem(word_ref[2] + turn + core * (ring // 2), ring) * block + start
            copied(
                part_ref, held_ref.at[pl.ds(pl.multiple_of(at, rows), rows), pl.ds(half, width)]
            )
        cols = pl.ds(pl.multiple_of(core * half, half), half)
        for source, left in ((query_ref, 0), (out_ref, half + width)):
            for side in range(2):
                first = pl.multiple_of(lax.rem(core + side, 2) * half, half)
                copied(
                    source.at[0, pl.ds(first, half), cols],
                    held_ref.at[pl.ds(side * half, half), pl.ds(left, half)],
                )
        for copy in copies:
            copy.start()
        gain_held[...] = gain_ref[0]
        next_gain_held[...] = next_gain_ref[0]

        def picked(table_ref, step, held):
            row = pl.ds(time_ref[step, word_ref[1]], 1)
            for third in range(3):
                for side in range(2):
                    first = (2 * third + lax.rem(core + side, 2)) * half
                    first = pl.ds(pl.multiple_of(first, half), half)
                    held[2 * third + side : 2 * third + side + 1, :] = table_ref[0, row, first]

        for step, held in enumerate(mods_held):
            picked(mod_ref, step, held)
        picked(next_mod_ref, len(mods_held) - 1, next_mods_held)
        for copy in copies:
            copy.wait()

    return body


def advance_slot(step):
    def body(word_ref, time_ref, size_ref, slot_ref, hidden_ref, out_ref):
        size = size_ref[time_ref[step, word_ref[1]]]
        out_ref[...] = (
            slot_ref[...].astype(jnp.float32) - size * hidden_ref[...].astype(jnp.float32)
        ).astype(jnp.bfloat16)

    return body


def finish(step, holder):
    def body(time_ref, size_ref, got_ref, out_ref):
        for micro in range(out_ref.shape[0]):
            size = size_ref[time_ref[step, micro]]
            slot = got_ref[0, micro].astype(jnp.float32)
            hidden = got_ref[holder, micro].astype(jnp.float32)
            out_ref[micro] = (slot - size * hidden).astype(jnp.bfloat16)

    return body


def shards(latents, timesteps, step_sizes, mod_table, qk_gain, w_query, w_kv, w_out):
    n_pipe = lax.axis_size("pipe")
    n_seq = lax.axis_size("seq")
    pipe_at = lax.axis_index("pipe")
    seq_at = lax.axis_index("seq")
    core = seq_at % 2
    micro = (seq_at // 2) % 2
    micro_count, row_share, feature_share = latents.shape
    step_count = timesteps.shape[0]
    tokens = row_share * n_seq
    width = feature_share * n_pipe
    half = width // 2
    head_dim = qk_gain.shape[2]
    core_pairs = [(at, at ^ 1) for at in range(n_seq)]
    quads = [[4 * at + j for j in range(4)] for at in range(n_seq // 4)]

    def swapped(value):
        return lax.ppermute(value, "seq", core_pairs)

    def columns(value, side, axis):
        return lax.dynamic_slice_in_dim(value, side * half, half, axis)

    def kv_columns(side):
        keys, values = w_kv[0, :, :width], w_kv[0, :, width:]
        return jnp.concatenate([columns(keys, side, 1), columns(values, side, 1)], axis=1)

    mine = kv_columns(core)
    theirs = swapped(kv_columns(1 - core))
    low = jnp.where(core == 0, mine, theirs)
    high = jnp.where(core == 0, theirs, mine)
    block = jnp.concatenate([low, high], axis=0)
    latents, block = lax.optimization_barrier((latents, block))
    theirs = lax.ppermute(block, "seq", [(at, at ^ 2) for at in range(n_seq)])

    sent = jnp.broadcast_to(latents[None], (n_pipe,) + latents.shape)
    rows = lax.all_to_all(sent, "pipe", 0, 0, tiled=True)
    low = jnp.where(micro == 0, block, theirs)
    high = jnp.where(micro == 0, theirs, block)
    block = jnp.concatenate([low, high], axis=0)
    backward = [(at + 1, at) for at in range(0, n_pipe, 2)]

    def to_even(value):
        return lax.ppermute(value, "pipe", backward)

    rows, block = lax.optimization_barrier((rows, block))
    ring = n_seq // 4
    rings = [[(at, (at + turn) % n_seq) for at in range(n_seq)] for turn in (4, -4)]
    middle = block.shape[0] // 2
    rising = falling = block
    parts = [block]
    spots = [(0, 0)]
    for turn in range(1, ring // 2):
        rising = lax.ppermute(rising, "seq", rings[0])
        falling = lax.ppermute(falling, "seq", rings[1])
        parts += [rising, falling]
        spots += [(ring - turn, 0), (turn, 0)]
        if turn == 1:
            rows, rising, falling = lax.optimization_barrier((rows, rising, falling))
    parts += [
        lax.ppermute(rising[:middle], "seq", rings[0]),
        lax.ppermute(falling[middle:], "seq", rings[1]),
    ]
    spots += [(ring // 2, 0), (ring // 2, middle)]

    rows = jnp.transpose(rows, (1, 2, 0, 3)).reshape(micro_count, row_share, 2, half)
    sent = jnp.transpose(rows, (0, 2, 1, 3)).reshape(1, 4, row_share, half)
    sent = jnp.broadcast_to(sent, (n_seq // 4, 4, row_share, half)).reshape(
        n_seq, row_share, half
    )
    slot = lax.all_to_all(sent, "seq", 0, 0, tiled=True).reshape(tokens, half)

    next_table, next_gain = to_even(mod_table), to_even(qk_gain)
    parts[-1], next_table, next_gain = lax.optimization_barrier(
        (parts[-1], next_table, next_gain)
    )
    words = jnp.stack([core, micro, seq_at // 4]).astype(jnp.int32)
    smem = pl.BlockSpec(memory_space=pltpu.SMEM)
    vmem = pl.BlockSpec(memory_space=pltpu.VMEM)
    hbm = pl.BlockSpec(memory_space=pltpu.HBM)
    held_shape = jax.ShapeDtypeStruct((width, 2 * width), jnp.bfloat16)
    small_shapes = [jax.ShapeDtypeStruct(qk_gain.shape[1:], jnp.float32)] * 2 + [
        jax.ShapeDtypeStruct((6, half), jnp.float32)
    ] * (1 + step_count)

    def in_hbm(value):
        return pltpu.with_memory_space_constraint(value, pltpu.HBM)

    loaded = pl.pallas_call(
        load_own(spots),
        out_shape=[held_shape] + small_shapes,
        in_specs=[smem] + [hbm] * len(parts) + [smem] + [vmem] * 4 + [hbm, hbm],
        out_specs=[vmem] * (4 + step_count),
        scratch_shapes=[pltpu.SemaphoreType.DMA((len(parts) + 4,))],
        compiler_params=pltpu.CompilerParams(vmem_limit_bytes=12 << 20),
        name="load_own",
    )(
        words,
        *(in_hbm(part) for part in parts),
        timesteps,
        mod_table,
        qk_gain,
        next_table,
        next_gain,
        in_hbm(w_query),
        in_hbm(w_out),
    )
    held, gains, next_gains, next_mods = loaded[:4]
    mods = loaded[4:]

    def layer(hidden, mods, gains, weights):
        attended = pl.pallas_call(
            layer_front(head_dim),
            out_shape=jax.ShapeDtypeStruct((tokens, half), jnp.bfloat16),
            in_specs=[vmem] * 5,
            out_specs=vmem,
            compiler_params=pltpu.CompilerParams(vmem_limit_bytes=16 << 20),
            name="front",
        )(hidden, swapped(hidden), mods, gains, weights)
        return pl.pallas_call(
            layer_back,
            out_shape=jax.ShapeDtypeStruct((tokens, half), jnp.bfloat16),
            in_specs=[vmem] * 5,
            out_specs=vmem,
            compiler_params=pltpu.CompilerParams(vmem_limit_bytes=12 << 20),
            name="back",
        )(attended, swapped(attended), hidden, mods, weights)

    following = [next_mods, next_gains, to_even(held)]

    holder = 0
    hidden = slot
    for step in range(step_count):
        for section in range(n_pipe):
            joined = step > 0
            place = section - section % 2 if joined else section
            if place != holder:
                hidden = lax.ppermute(hidden, "pipe", [(holder, place)])
                holder = place
            if step > 0 and section == 0:
                hidden, following[2] = lax.optimization_barrier((hidden, following[2]))
                slot = pl.pallas_call(
                    advance_slot(step - 1),
                    out_shape=jax.ShapeDtypeStruct((tokens, half), jnp.bfloat16),
                    in_specs=[smem] * 3 + [vmem] * 2,
                    out_specs=vmem,
                    compiler_params=pltpu.CompilerParams(vmem_limit_bytes=8 << 20),
                    name="advance_slot",
                )(words, timesteps, step_sizes, slot, hidden)
                hidden = slot
            hidden = layer(hidden, *(following if section != place else (mods[step], gains, held)))

    kept = jnp.where(pipe_at == 0, slot, hidden)
    kept = lax.dynamic_slice_in_dim(kept, (seq_at // 4) * 4 * row_share, 4 * row_share, 0)
    kept = kept.reshape(4, row_share, half)
    kept = lax.all_to_all(kept, "seq", 0, 0, tiled=True, axis_index_groups=quads)
    kept = kept.reshape(micro_count, 2, row_share, n_pipe // 2, feature_share)
    sent = jnp.transpose(kept, (1, 3, 0, 2, 4)).reshape(
        n_pipe, micro_count, row_share, feature_share
    )
    got = lax.all_to_all(sent, "pipe", 0, 0, tiled=True)
    return pl.pallas_call(
        finish(step_count - 1, holder),
        out_shape=jax.ShapeDtypeStruct(latents.shape, jnp.bfloat16),
        in_specs=[smem] * 2 + [vmem],
        out_specs=vmem,
        compiler_params=pltpu.CompilerParams(vmem_limit_bytes=8 << 20),
        name="finish",
    )(timesteps, step_sizes, got)


def solution(mesh):
    in_specs = (
        P(None, "seq", "pipe"),
        P(),
        P(),
        P("pipe", None, None),
        P("pipe", None, None),
        P("pipe", None, None),
        P("pipe", "seq", None),
        P("pipe", None, None),
    )
    out_specs = P(None, "seq", "pipe")
    return jax.shard_map(shards, mesh=mesh, in_specs=in_specs, out_specs=out_specs, check_vma=False)
```

```python
import math

import jax
import jax.numpy as jnp
from jax import lax
from jax.experimental import pallas as pl
from jax.experimental.pallas import tpu as pltpu
from jax.sharding import PartitionSpec as P

norm_eps = 1e-06


def layer_front(head_dim):
    score_scale = 1.0 / math.sqrt(head_dim)

    def body(own_ref, other_ref, mod_ref, gain_ref, sides_ref, kv_ref, out_ref):
        half = own_ref.shape[1]
        width = 2 * half
        own = own_ref[...].astype(jnp.float32)
        other = other_ref[...].astype(jnp.float32)
        center = (
            jnp.sum(own, axis=-1, keepdims=True) + jnp.sum(other, axis=-1, keepdims=True)
        ) / width
        own = own - center
        other = other - center
        spread = (
            jnp.sum(own * own, axis=-1, keepdims=True)
            + jnp.sum(other * other, axis=-1, keepdims=True)
        ) / width
        inverse = lax.rsqrt(spread + norm_eps)

        def modulated(values, at):
            shift_row = mod_ref[at : at + 1, :]
            scale_row = mod_ref[2 + at : 3 + at, :]
            return (values * inverse * (1.0 + scale_row) + shift_row).astype(jnp.bfloat16)

        own = modulated(own, 0)
        other = modulated(other, 1)

        def project(weight_ref, start, size):
            cols = slice(start, start + size)
            return jnp.dot(
                own, weight_ref[:half, cols], preferred_element_type=jnp.float32
            ) + jnp.dot(other, weight_ref[half:, cols], preferred_element_type=jnp.float32)

        def rms(values, gain_row):
            mean_square = jnp.mean(values * values, axis=-1, keepdims=True)
            return (values * lax.rsqrt(mean_square + norm_eps) * gain_row).astype(jnp.bfloat16)

        gain_query = gain_ref[0:1, :]
        gain_key = gain_ref[1:2, :]
        group = 2 * head_dim
        for start in range(0, half, group):
            queries = project(sides_ref, start, group)
            keys = project(kv_ref, start, group)
            values = project(kv_ref, half + start, group).astype(jnp.bfloat16)
            for at in range(0, group, head_dim):
                query_head = rms(queries[:, at : at + head_dim], gain_query)
                key_head = rms(keys[:, at : at + head_dim], gain_key)
                logits = (
                    lax.dot_general(
                        query_head,
                        key_head,
                        (((1,), (1,)), ((), ())),
                        preferred_element_type=jnp.float32,
                    )
                    * score_scale
                )
                weights = jnp.exp(logits)
                total = jnp.sum(weights, axis=-1, keepdims=True)
                mixed = jnp.dot(
                    weights.astype(jnp.bfloat16),
                    values[:, at : at + head_dim],
                    preferred_element_type=jnp.float32,
                )
                out_ref[:, start + at : start + at + head_dim] = (mixed / total).astype(
                    jnp.bfloat16
                )

    return body


def layer_back(own_ref, other_ref, hidden_ref, mod_ref, weight_ref, out_ref):
    half = own_ref.shape[1]
    cols = slice(half, 2 * half)
    projected = jnp.dot(
        own_ref[...], weight_ref[:half, cols], preferred_element_type=jnp.float32
    ) + jnp.dot(other_ref[...], weight_ref[half:, cols], preferred_element_type=jnp.float32)
    out_ref[...] = (
        hidden_ref[...].astype(jnp.float32) + mod_ref[4:5, :] * projected
    ).astype(jnp.bfloat16)


def load_own(spots):
    def body(word_ref, *refs):
        part_refs = refs[: len(spots)]
        time_ref, mod_ref, gain_ref, next_mod_ref, next_gain_ref, query_ref, out_ref = refs[
            len(spots) : len(spots) + 7
        ]
        sides_held, kv_held, gain_held, next_gain_held, next_mods_held = refs[
            len(spots) + 7 : len(spots) + 12
        ]
        mods_held, sems = refs[len(spots) + 12 : -1], refs[-1]
        core = word_ref[0]
        width = kv_held.shape[0]
        half = width // 2
        block = part_refs[0].shape[0]
        ring = width // block
        copies = []

        def copied(source, target):
            copies.append(pltpu.make_async_copy(source, target, sems.at[len(copies)]))

        for (turn, start), part_ref in zip(spots, part_refs):
            rows = part_ref.shape[0]
            at = lax.rem(word_ref[2] + turn + core * (ring // 2), ring) * block + start
            copied(part_ref, kv_held.at[pl.ds(pl.multiple_of(at, rows), rows), :])
        cols = pl.ds(pl.multiple_of(core * half, half), half)
        for source, left in ((query_ref, 0), (out_ref, half)):
            for side in range(2):
                first = pl.multiple_of(lax.rem(core + side, 2) * half, half)
                copied(
                    source.at[0, pl.ds(first, half), cols],
                    sides_held.at[pl.ds(side * half, half), pl.ds(left, half)],
                )
        for copy in copies:
            copy.start()
        gain_held[...] = gain_ref[0]
        next_gain_held[...] = next_gain_ref[0]

        def picked(table_ref, step, held):
            row = pl.ds(time_ref[step, word_ref[1]], 1)
            for third in range(3):
                for side in range(2):
                    first = (2 * third + lax.rem(core + side, 2)) * half
                    first = pl.ds(pl.multiple_of(first, half), half)
                    held[2 * third + side : 2 * third + side + 1, :] = table_ref[0, row, first]

        for step, held in enumerate(mods_held):
            picked(mod_ref, step, held)
        picked(next_mod_ref, len(mods_held) - 1, next_mods_held)
        for copy in copies:
            copy.wait()

    return body


def advance_slot(step):
    def body(word_ref, time_ref, size_ref, slot_ref, hidden_ref, out_ref):
        size = size_ref[time_ref[step, word_ref[1]]]
        out_ref[...] = (
            slot_ref[...].astype(jnp.float32) - size * hidden_ref[...].astype(jnp.float32)
        ).astype(jnp.bfloat16)

    return body


def finish(step, holder):
    def body(time_ref, size_ref, got_ref, out_ref):
        for micro in range(out_ref.shape[0]):
            size = size_ref[time_ref[step, micro]]
            slot = got_ref[0, micro].astype(jnp.float32)
            hidden = got_ref[holder, micro].astype(jnp.float32)
            out_ref[micro] = (slot - size * hidden).astype(jnp.bfloat16)

    return body


def shards(latents, timesteps, step_sizes, mod_table, qk_gain, w_query, w_kv, w_out):
    n_pipe = lax.axis_size("pipe")
    n_seq = lax.axis_size("seq")
    pipe_at = lax.axis_index("pipe")
    seq_at = lax.axis_index("seq")
    core = seq_at % 2
    micro = (seq_at // 2) % 2
    micro_count, row_share, feature_share = latents.shape
    step_count = timesteps.shape[0]
    tokens = row_share * n_seq
    width = feature_share * n_pipe
    half = width // 2
    head_dim = qk_gain.shape[2]
    core_pairs = [(at, at ^ 1) for at in range(n_seq)]
    octets = [[8 * at + j for j in range(8)] for at in range(n_seq // 8)]

    def swapped(value):
        return lax.ppermute(value, "seq", core_pairs)

    def columns(value, side, axis):
        return lax.dynamic_slice_in_dim(value, side * half, half, axis)

    def kv_columns(side):
        keys, values = w_kv[0, :, :width], w_kv[0, :, width:]
        return jnp.concatenate([columns(keys, side, 1), columns(values, side, 1)], axis=1)

    mine = kv_columns(core)
    theirs = swapped(kv_columns(1 - core))
    low = jnp.where(core == 0, mine, theirs)
    high = jnp.where(core == 0, theirs, mine)
    block = jnp.concatenate([low, high], axis=0)
    latents, block = lax.optimization_barrier((latents, block))
    theirs = lax.ppermute(block, "seq", [(at, at ^ 2) for at in range(n_seq)])

    sent = jnp.broadcast_to(latents[None], (n_pipe,) + latents.shape)
    rows = lax.all_to_all(sent, "pipe", 0, 0, tiled=True)
    low = jnp.where(micro == 0, block, theirs)
    high = jnp.where(micro == 0, theirs, block)
    block = jnp.concatenate([low, high], axis=0)
    backward = [(at + 1, at) for at in range(0, n_pipe, 2)]

    def to_even(value):
        return lax.ppermute(value, "pipe", backward)

    rows, block = lax.optimization_barrier((rows, block))
    ring = n_seq // 4
    rings = [[(at, (at + turn) % n_seq) for at in range(n_seq)] for turn in (4, -4)]
    middle = block.shape[0] // 2
    rising = falling = block
    parts = [block]
    spots = [(0, 0)]
    for turn in range(1, ring // 2):
        rising = lax.ppermute(rising, "seq", rings[0])
        falling = lax.ppermute(falling, "seq", rings[1])
        parts += [rising, falling]
        spots += [(ring - turn, 0), (turn, 0)]
        if turn == 1:
            rows, rising, falling = lax.optimization_barrier((rows, rising, falling))
    parts += [
        lax.ppermute(rising[:middle], "seq", rings[0]),
        lax.ppermute(falling[middle:], "seq", rings[1]),
    ]
    spots += [(ring // 2, 0), (ring // 2, middle)]

    rows = jnp.transpose(rows, (1, 2, 0, 3)).reshape(micro_count, row_share, 2, half)
    sent = jnp.transpose(rows, (0, 2, 1, 3)).reshape(1, 4, row_share, half)
    sent = jnp.broadcast_to(sent, (n_seq // 4, 4, row_share, half)).reshape(
        n_seq, row_share, half
    )
    slot = lax.all_to_all(sent, "seq", 0, 0, tiled=True).reshape(tokens, half)

    next_table, next_gain = to_even(mod_table), to_even(qk_gain)
    parts[-1], next_table, next_gain = lax.optimization_barrier(
        (parts[-1], next_table, next_gain)
    )
    words = jnp.stack([core, micro, seq_at // 4]).astype(jnp.int32)
    smem = pl.BlockSpec(memory_space=pltpu.SMEM)
    vmem = pl.BlockSpec(memory_space=pltpu.VMEM)
    hbm = pl.BlockSpec(memory_space=pltpu.HBM)
    held_shape = jax.ShapeDtypeStruct((width, width), jnp.bfloat16)
    small_shapes = [jax.ShapeDtypeStruct(qk_gain.shape[1:], jnp.float32)] * 2 + [
        jax.ShapeDtypeStruct((6, half), jnp.float32)
    ] * (1 + step_count)

    def in_hbm(value):
        return pltpu.with_memory_space_constraint(value, pltpu.HBM)

    loaded = pl.pallas_call(
        load_own(spots),
        out_shape=[held_shape] * 2 + small_shapes,
        in_specs=[smem] + [hbm] * len(parts) + [smem] + [vmem] * 4 + [hbm, hbm],
        out_specs=[vmem] * (5 + step_count),
        scratch_shapes=[pltpu.SemaphoreType.DMA((len(parts) + 4,))],
        compiler_params=pltpu.CompilerParams(vmem_limit_bytes=12 << 20),
        name="load_own",
    )(
        words,
        *(in_hbm(part) for part in parts),
        timesteps,
        mod_table,
        qk_gain,
        next_table,
        next_gain,
        in_hbm(w_query),
        in_hbm(w_out),
    )
    sides, kv, gains, next_gains, next_mods = loaded[:5]
    mods = loaded[5:]

    def layer(hidden, mods, gains, sides, kv):
        attended = pl.pallas_call(
            layer_front(head_dim),
            out_shape=jax.ShapeDtypeStruct((tokens, half), jnp.bfloat16),
            in_specs=[vmem] * 6,
            out_specs=vmem,
            compiler_params=pltpu.CompilerParams(vmem_limit_bytes=16 << 20),
            name="front",
        )(hidden, swapped(hidden), mods, gains, sides, kv)
        return pl.pallas_call(
            layer_back,
            out_shape=jax.ShapeDtypeStruct((tokens, half), jnp.bfloat16),
            in_specs=[vmem] * 5,
            out_specs=vmem,
            compiler_params=pltpu.CompilerParams(vmem_limit_bytes=12 << 20),
            name="back",
        )(attended, swapped(attended), hidden, mods, sides)

    evens = [at for at in range(n_seq) if at // 4 % 2 == 0]

    def pairs_from(shift):
        return [
            ((place + 1) * n_seq + at + shift, place * n_seq + at)
            for place in range(0, n_pipe, 2)
            for at in evens
        ]

    next_sides = lax.ppermute(sides, ("pipe", "seq"), pairs_from(0))
    next_kv = lax.ppermute(kv, ("pipe", "seq"), pairs_from(4))

    holder = 0
    hidden = slot
    for step in range(step_count):
        for section in range(n_pipe):
            joined = step > 0
            place = section - section % 2 if joined else section
            if place != holder:
                hidden = lax.ppermute(hidden, "pipe", [(holder, place)])
                holder = place
            if step > 0 and section == 0:
                slot = pl.pallas_call(
                    advance_slot(step - 1),
                    out_shape=jax.ShapeDtypeStruct((tokens, half), jnp.bfloat16),
                    in_specs=[smem] * 3 + [vmem] * 2,
                    out_specs=vmem,
                    compiler_params=pltpu.CompilerParams(vmem_limit_bytes=8 << 20),
                    name="advance_slot",
                )(words, timesteps, step_sizes, slot, hidden)
                hidden = slot
            if section == place:
                weights = (mods[step], gains, sides, kv)
            else:
                weights = (next_mods, next_gains, next_sides, next_kv)
            hidden = layer(hidden, *weights)
            if step == 0 and section == n_pipe - 1:
                hidden, next_sides, next_kv = lax.optimization_barrier(
                    (hidden, next_sides, next_kv)
                )

    kept = jnp.where(pipe_at == 0, slot, hidden)
    kept = lax.dynamic_slice_in_dim(kept, (seq_at // 8) * 8 * row_share, 8 * row_share, 0)
    kept = kept.reshape(8, row_share, half)
    kept = lax.all_to_all(kept, "seq", 0, 0, tiled=True, axis_index_groups=octets)[:4]
    kept = kept.reshape(micro_count, 2, row_share, n_pipe // 2, feature_share)
    sent = jnp.transpose(kept, (1, 3, 0, 2, 4)).reshape(
        n_pipe, micro_count, row_share, feature_share
    )
    got = lax.all_to_all(sent, "pipe", 0, 0, tiled=True)
    return pl.pallas_call(
        finish(step_count - 1, holder),
        out_shape=jax.ShapeDtypeStruct(latents.shape, jnp.bfloat16),
        in_specs=[smem] * 2 + [vmem],
        out_specs=vmem,
        compiler_params=pltpu.CompilerParams(vmem_limit_bytes=8 << 20),
        name="finish",
    )(timesteps, step_sizes, got)


def solution(mesh):
    in_specs = (
        P(None, "seq", "pipe"),
        P(),
        P(),
        P("pipe", None, None),
        P("pipe", None, None),
        P("pipe", None, None),
        P("pipe", "seq", None),
        P("pipe", None, None),
    )
    out_specs = P(None, "seq", "pipe")
    return jax.shard_map(shards, mesh=mesh, in_specs=in_specs, out_specs=out_specs, check_vma=False)
```

```python
import math

import jax
import jax.numpy as jnp
from jax import lax
from jax.experimental import pallas as pl
from jax.experimental.pallas import tpu as pltpu
from jax.sharding import PartitionSpec as P

norm_eps = 1e-06


def layer_front(head_dim):
    score_scale = 1.0 / math.sqrt(head_dim)

    def body(own_ref, other_ref, mod_ref, gain_ref, weight_ref, out_ref):
        half = own_ref.shape[1]
        width = 2 * half
        own = own_ref[...].astype(jnp.float32)
        other = other_ref[...].astype(jnp.float32)
        center = (
            jnp.sum(own, axis=-1, keepdims=True) + jnp.sum(other, axis=-1, keepdims=True)
        ) / width
        own = own - center
        other = other - center
        spread = (
            jnp.sum(own * own, axis=-1, keepdims=True)
            + jnp.sum(other * other, axis=-1, keepdims=True)
        ) / width
        inverse = lax.rsqrt(spread + norm_eps)

        def modulated(values, at):
            shift_row = mod_ref[at : at + 1, :]
            scale_row = mod_ref[2 + at : 3 + at, :]
            return (values * inverse * (1.0 + scale_row) + shift_row).astype(jnp.bfloat16)

        own = modulated(own, 0)
        other = modulated(other, 1)

        def project(start, size):
            cols = slice(start, start + size)
            return jnp.dot(
                own, weight_ref[:half, cols], preferred_element_type=jnp.float32
            ) + jnp.dot(other, weight_ref[half:, cols], preferred_element_type=jnp.float32)

        def rms(values, gain_row):
            mean_square = jnp.mean(values * values, axis=-1, keepdims=True)
            return (values * lax.rsqrt(mean_square + norm_eps) * gain_row).astype(jnp.bfloat16)

        gain_query = gain_ref[0:1, :]
        gain_key = gain_ref[1:2, :]
        group = 2 * head_dim
        for start in range(0, half, group):
            queries = project(start, group)
            keys = project(half + start, group)
            values = project(2 * half + start, group).astype(jnp.bfloat16)
            for at in range(0, group, head_dim):
                query_head = rms(queries[:, at : at + head_dim], gain_query)
                key_head = rms(keys[:, at : at + head_dim], gain_key)
                logits = (
                    lax.dot_general(
                        query_head,
                        key_head,
                        (((1,), (1,)), ((), ())),
                        preferred_element_type=jnp.float32,
                    )
                    * score_scale
                )
                weights = jnp.exp(logits)
                total = jnp.sum(weights, axis=-1, keepdims=True)
                mixed = jnp.dot(
                    weights.astype(jnp.bfloat16),
                    values[:, at : at + head_dim],
                    preferred_element_type=jnp.float32,
                )
                out_ref[:, start + at : start + at + head_dim] = (mixed / total).astype(
                    jnp.bfloat16
                )

    return body


def layer_back(own_ref, other_ref, hidden_ref, mod_ref, weight_ref, out_ref):
    half = own_ref.shape[1]
    cols = slice(3 * half, 4 * half)
    projected = jnp.dot(
        own_ref[...], weight_ref[:half, cols], preferred_element_type=jnp.float32
    ) + jnp.dot(other_ref[...], weight_ref[half:, cols], preferred_element_type=jnp.float32)
    out_ref[...] = (
        hidden_ref[...].astype(jnp.float32) + mod_ref[4:5, :] * projected
    ).astype(jnp.bfloat16)


def load_own(spots):
    def body(word_ref, *refs):
        part_refs = refs[: len(spots)]
        time_ref, mod_ref, gain_ref, next_mod_ref, next_gain_ref, query_ref, out_ref = refs[
            len(spots) : len(spots) + 7
        ]
        held_ref, gain_held, next_gain_held, next_mods_held = refs[
            len(spots) + 7 : len(spots) + 11
        ]
        mods_held, sems = refs[len(spots) + 11 : -1], refs[-1]
        core = word_ref[0]
        width = held_ref.shape[0]
        half = width // 2
        block = part_refs[0].shape[0]
        ring = width // block
        copies = []

        def copied(source, target):
            copies.append(pltpu.make_async_copy(source, target, sems.at[len(copies)]))

        for (turn, start), part_ref in zip(spots, part_refs):
            rows = part_ref.shape[0]
            at = lax.rem(word_ref[2] + turn + core * (ring // 2), ring) * block + start
            copied(
                part_ref, held_ref.at[pl.ds(pl.multiple_of(at, rows), rows), pl.ds(half, width)]
            )
        cols = pl.ds(pl.multiple_of(core * half, half), half)
        for source, left in ((query_ref, 0), (out_ref, half + width)):
            for side in range(2):
                first = pl.multiple_of(lax.rem(core + side, 2) * half, half)
                copied(
                    source.at[0, pl.ds(first, half), cols],
                    held_ref.at[pl.ds(side * half, half), pl.ds(left, half)],
                )
        for copy in copies:
            copy.start()
        gain_held[...] = gain_ref[0]
        next_gain_held[...] = next_gain_ref[0]

        def picked(table_ref, step, held):
            row = pl.ds(time_ref[step, word_ref[1]], 1)
            for third in range(3):
                for side in range(2):
                    first = (2 * third + lax.rem(core + side, 2)) * half
                    first = pl.ds(pl.multiple_of(first, half), half)
                    held[2 * third + side : 2 * third + side + 1, :] = table_ref[0, row, first]

        for step, held in enumerate(mods_held):
            picked(mod_ref, step, held)
        picked(next_mod_ref, len(mods_held) - 1, next_mods_held)
        for copy in copies:
            copy.wait()

    return body


def advance_slot(step):
    def body(word_ref, time_ref, size_ref, slot_ref, hidden_ref, out_ref):
        size = size_ref[time_ref[step, word_ref[1]]]
        out_ref[...] = (
            slot_ref[...].astype(jnp.float32) - size * hidden_ref[...].astype(jnp.float32)
        ).astype(jnp.bfloat16)

    return body


def finish(step, holder):
    def body(time_ref, size_ref, got_ref, out_ref):
        for micro in range(out_ref.shape[0]):
            size = size_ref[time_ref[step, micro]]
            slot = got_ref[0, micro].astype(jnp.float32)
            hidden = got_ref[holder, micro].astype(jnp.float32)
            out_ref[micro] = (slot - size * hidden).astype(jnp.bfloat16)

    return body


def shards(latents, timesteps, step_sizes, mod_table, qk_gain, w_query, w_kv, w_out):
    n_pipe = lax.axis_size("pipe")
    n_seq = lax.axis_size("seq")
    pipe_at = lax.axis_index("pipe")
    seq_at = lax.axis_index("seq")
    core = seq_at % 2
    micro = (seq_at // 2) % 2
    micro_count, row_share, feature_share = latents.shape
    step_count = timesteps.shape[0]
    tokens = row_share * n_seq
    width = feature_share * n_pipe
    half = width // 2
    head_dim = qk_gain.shape[2]
    core_pairs = [(at, at ^ 1) for at in range(n_seq)]
    quads = [[4 * at + j for j in range(4)] for at in range(n_seq // 4)]

    def swapped(value):
        return lax.ppermute(value, "seq", core_pairs)

    def columns(value, side, axis):
        return lax.dynamic_slice_in_dim(value, side * half, half, axis)

    def kv_columns(side):
        keys, values = w_kv[0, :, :width], w_kv[0, :, width:]
        return jnp.concatenate([columns(keys, side, 1), columns(values, side, 1)], axis=1)

    mine = kv_columns(core)
    theirs = swapped(kv_columns(1 - core))
    low = jnp.where(core == 0, mine, theirs)
    high = jnp.where(core == 0, theirs, mine)
    block = jnp.concatenate([low, high], axis=0)
    latents, block = lax.optimization_barrier((latents, block))
    theirs = lax.ppermute(block, "seq", [(at, at ^ 2) for at in range(n_seq)])

    sent = jnp.broadcast_to(latents[None], (n_pipe,) + latents.shape)
    rows = lax.all_to_all(sent, "pipe", 0, 0, tiled=True)
    low = jnp.where(micro == 0, block, theirs)
    high = jnp.where(micro == 0, theirs, block)
    block = jnp.concatenate([low, high], axis=0)
    backward = [(at + 1, at) for at in range(0, n_pipe, 2)]

    def to_even(value):
        return lax.ppermute(value, "pipe", backward)

    rows, block = lax.optimization_barrier((rows, block))
    ring = n_seq // 4
    rings = [[(at, (at + turn) % n_seq) for at in range(n_seq)] for turn in (4, -4)]
    middle = block.shape[0] // 2
    rising = falling = block
    parts = [block]
    spots = [(0, 0)]
    for turn in range(1, ring // 2):
        rising = lax.ppermute(rising, "seq", rings[0])
        falling = lax.ppermute(falling, "seq", rings[1])
        parts += [rising, falling]
        spots += [(ring - turn, 0), (turn, 0)]
        if turn == 1:
            rows, rising, falling = lax.optimization_barrier((rows, rising, falling))
    parts += [
        lax.ppermute(rising[:middle], "seq", rings[0]),
        lax.ppermute(falling[middle:], "seq", rings[1]),
    ]
    spots += [(ring // 2, 0), (ring // 2, middle)]

    rows = jnp.transpose(rows, (1, 2, 0, 3)).reshape(micro_count, row_share, 2, half)
    sent = jnp.transpose(rows, (0, 2, 1, 3)).reshape(1, 4, row_share, half)
    sent = jnp.broadcast_to(sent, (n_seq // 4, 4, row_share, half)).reshape(
        n_seq, row_share, half
    )
    slot = lax.all_to_all(sent, "seq", 0, 0, tiled=True).reshape(tokens, half)

    next_table, next_gain = to_even(mod_table), to_even(qk_gain)
    parts[-1], next_table, next_gain = lax.optimization_barrier(
        (parts[-1], next_table, next_gain)
    )
    words = jnp.stack([core, micro, seq_at // 4]).astype(jnp.int32)
    smem = pl.BlockSpec(memory_space=pltpu.SMEM)
    vmem = pl.BlockSpec(memory_space=pltpu.VMEM)
    hbm = pl.BlockSpec(memory_space=pltpu.HBM)
    held_shape = jax.ShapeDtypeStruct((width, 2 * width), jnp.bfloat16)
    small_shapes = [jax.ShapeDtypeStruct(qk_gain.shape[1:], jnp.float32)] * 2 + [
        jax.ShapeDtypeStruct((6, half), jnp.float32)
    ] * (1 + step_count)

    def in_hbm(value):
        return pltpu.with_memory_space_constraint(value, pltpu.HBM)

    loaded = pl.pallas_call(
        load_own(spots),
        out_shape=[held_shape] + small_shapes,
        in_specs=[smem] + [hbm] * len(parts) + [smem] + [vmem] * 4 + [hbm, hbm],
        out_specs=[vmem] * (4 + step_count),
        scratch_shapes=[pltpu.SemaphoreType.DMA((len(parts) + 4,))],
        compiler_params=pltpu.CompilerParams(vmem_limit_bytes=12 << 20),
        name="load_own",
    )(
        words,
        *(in_hbm(part) for part in parts),
        timesteps,
        mod_table,
        qk_gain,
        next_table,
        next_gain,
        in_hbm(w_query),
        in_hbm(w_out),
    )
    held, gains, next_gains, next_mods = loaded[:4]
    mods = loaded[4:]

    def layer(hidden, mods, gains, weights):
        attended = pl.pallas_call(
            layer_front(head_dim),
            out_shape=jax.ShapeDtypeStruct((tokens, half), jnp.bfloat16),
            in_specs=[vmem] * 5,
            out_specs=vmem,
            compiler_params=pltpu.CompilerParams(vmem_limit_bytes=16 << 20),
            name="front",
        )(hidden, swapped(hidden), mods, gains, weights)
        return pl.pallas_call(
            layer_back,
            out_shape=jax.ShapeDtypeStruct((tokens, half), jnp.bfloat16),
            in_specs=[vmem] * 5,
            out_specs=vmem,
            compiler_params=pltpu.CompilerParams(vmem_limit_bytes=12 << 20),
            name="back",
        )(attended, swapped(attended), hidden, mods, weights)

    apart = 2
    held_pairs = [(at + 1, at) for at in range(apart, n_pipe, 2)]
    following = [next_mods, next_gains, lax.ppermute(held, "pipe", held_pairs)]

    holder = 0
    hidden = slot
    for step in range(step_count):
        for section in range(n_pipe):
            joined = step > 0 and section >= apart
            place = section - section % 2 if joined else section
            if place != holder:
                hidden = lax.ppermute(hidden, "pipe", [(holder, place)])
                holder = place
            if step > 0 and section == 0:
                hidden, following[2] = lax.optimization_barrier((hidden, following[2]))
                slot = pl.pallas_call(
                    advance_slot(step - 1),
                    out_shape=jax.ShapeDtypeStruct((tokens, half), jnp.bfloat16),
                    in_specs=[smem] * 3 + [vmem] * 2,
                    out_specs=vmem,
                    compiler_params=pltpu.CompilerParams(vmem_limit_bytes=8 << 20),
                    name="advance_slot",
                )(words, timesteps, step_sizes, slot, hidden)
                hidden = slot
            hidden = layer(hidden, *(following if section != place else (mods[step], gains, held)))

    kept = jnp.where(pipe_at == 0, slot, hidden)
    kept = lax.dynamic_slice_in_dim(kept, (seq_at // 4) * 4 * row_share, 4 * row_share, 0)
    kept = kept.reshape(4, row_share, half)
    kept = lax.all_to_all(kept, "seq", 0, 0, tiled=True, axis_index_groups=quads)
    kept = kept.reshape(micro_count, 2, row_share, n_pipe // 2, feature_share)
    sent = jnp.transpose(kept, (1, 3, 0, 2, 4)).reshape(
        n_pipe, micro_count, row_share, feature_share
    )
    got = lax.all_to_all(sent, "pipe", 0, 0, tiled=True)
    return pl.pallas_call(
        finish(step_count - 1, holder),
        out_shape=jax.ShapeDtypeStruct(latents.shape, jnp.bfloat16),
        in_specs=[smem] * 2 + [vmem],
        out_specs=vmem,
        compiler_params=pltpu.CompilerParams(vmem_limit_bytes=8 << 20),
        name="finish",
    )(timesteps, step_sizes, got)


def solution(mesh):
    in_specs = (
        P(None, "seq", "pipe"),
        P(),
        P(),
        P("pipe", None, None),
        P("pipe", None, None),
        P("pipe", None, None),
        P("pipe", "seq", None),
        P("pipe", None, None),
    )
    out_specs = P(None, "seq", "pipe")
    return jax.shard_map(shards, mesh=mesh, in_specs=in_specs, out_specs=out_specs, check_vma=False)
```

```python
import math

import jax
import jax.numpy as jnp
from jax import lax
from jax.experimental import pallas as pl
from jax.experimental.pallas import tpu as pltpu
from jax.sharding import PartitionSpec as P

norm_eps = 1e-06


def layer_front(head_dim):
    score_scale = 1.0 / math.sqrt(head_dim)

    def body(own_ref, other_ref, mod_ref, gain_ref, weight_ref, out_ref):
        half = own_ref.shape[1]
        width = 2 * half
        own = own_ref[...].astype(jnp.float32)
        other = other_ref[...].astype(jnp.float32)
        center = (
            jnp.sum(own, axis=-1, keepdims=True) + jnp.sum(other, axis=-1, keepdims=True)
        ) / width
        own = own - center
        other = other - center
        spread = (
            jnp.sum(own * own, axis=-1, keepdims=True)
            + jnp.sum(other * other, axis=-1, keepdims=True)
        ) / width
        inverse = lax.rsqrt(spread + norm_eps)

        def modulated(values, at):
            shift_row = mod_ref[at : at + 1, :]
            scale_row = mod_ref[2 + at : 3 + at, :]
            return (values * inverse * (1.0 + scale_row) + shift_row).astype(jnp.bfloat16)

        own = modulated(own, 0)
        other = modulated(other, 1)

        def project(start, size):
            cols = slice(start, start + size)
            return jnp.dot(
                own, weight_ref[:half, cols], preferred_element_type=jnp.float32
            ) + jnp.dot(other, weight_ref[half:, cols], preferred_element_type=jnp.float32)

        def rms(values, gain_row):
            mean_square = jnp.mean(values * values, axis=-1, keepdims=True)
            return (values * lax.rsqrt(mean_square + norm_eps) * gain_row).astype(jnp.bfloat16)

        gain_query = gain_ref[0:1, :]
        gain_key = gain_ref[1:2, :]
        group = 2 * head_dim
        for start in range(0, half, group):
            queries = project(start, group)
            keys = project(half + start, group)
            values = project(2 * half + start, group).astype(jnp.bfloat16)
            for at in range(0, group, head_dim):
                query_head = rms(queries[:, at : at + head_dim], gain_query)
                key_head = rms(keys[:, at : at + head_dim], gain_key)
                logits = (
                    lax.dot_general(
                        query_head,
                        key_head,
                        (((1,), (1,)), ((), ())),
                        preferred_element_type=jnp.float32,
                    )
                    * score_scale
                )
                weights = jnp.exp(logits)
                total = jnp.sum(weights, axis=-1, keepdims=True)
                mixed = jnp.dot(
                    weights.astype(jnp.bfloat16),
                    values[:, at : at + head_dim],
                    preferred_element_type=jnp.float32,
                )
                out_ref[:, start + at : start + at + head_dim] = (mixed / total).astype(
                    jnp.bfloat16
                )

    return body


def layer_back(own_ref, other_ref, hidden_ref, mod_ref, weight_ref, out_ref):
    half = own_ref.shape[1]
    cols = slice(3 * half, 4 * half)
    projected = jnp.dot(
        own_ref[...], weight_ref[:half, cols], preferred_element_type=jnp.float32
    ) + jnp.dot(other_ref[...], weight_ref[half:, cols], preferred_element_type=jnp.float32)
    out_ref[...] = (
        hidden_ref[...].astype(jnp.float32) + mod_ref[4:5, :] * projected
    ).astype(jnp.bfloat16)


def load_own(spots):
    def body(word_ref, *refs):
        part_refs = refs[: len(spots)]
        time_ref, mod_ref, gain_ref, next_mod_ref, next_gain_ref, query_ref, out_ref = refs[
            len(spots) : len(spots) + 7
        ]
        held_ref, gain_held, next_gain_held, next_mods_held = refs[
            len(spots) + 7 : len(spots) + 11
        ]
        mods_held, sems = refs[len(spots) + 11 : -1], refs[-1]
        core = word_ref[0]
        width = held_ref.shape[0]
        half = width // 2
        block = part_refs[0].shape[0]
        ring = width // block
        copies = []

        def copied(source, target):
            copies.append(pltpu.make_async_copy(source, target, sems.at[len(copies)]))

        for (turn, start), part_ref in zip(spots, part_refs):
            rows = part_ref.shape[0]
            at = lax.rem(word_ref[2] + turn + core * (ring // 2), ring) * block + start
            copied(
                part_ref, held_ref.at[pl.ds(pl.multiple_of(at, rows), rows), pl.ds(half, width)]
            )
        cols = pl.ds(pl.multiple_of(core * half, half), half)
        for source, left in ((query_ref, 0), (out_ref, half + width)):
            for side in range(2):
                first = pl.multiple_of(lax.rem(core + side, 2) * half, half)
                copied(
                    source.at[0, pl.ds(first, half), cols],
                    held_ref.at[pl.ds(side * half, half), pl.ds(left, half)],
                )
        for copy in copies:
            copy.start()
        gain_held[...] = gain_ref[0]
        next_gain_held[...] = next_gain_ref[0]

        def picked(table_ref, step, held):
            row = pl.ds(time_ref[step, word_ref[1]], 1)
            for third in range(3):
                for side in range(2):
                    first = (2 * third + lax.rem(core + side, 2)) * half
                    first = pl.ds(pl.multiple_of(first, half), half)
                    held[2 * third + side : 2 * third + side + 1, :] = table_ref[0, row, first]

        for step, held in enumerate(mods_held):
            picked(mod_ref, step, held)
        picked(next_mod_ref, len(mods_held) - 1, next_mods_held)
        for copy in copies:
            copy.wait()

    return body


def advance_slot(step):
    def body(word_ref, time_ref, size_ref, slot_ref, hidden_ref, out_ref):
        size = size_ref[time_ref[step, word_ref[1]]]
        out_ref[...] = (
            slot_ref[...].astype(jnp.float32) - size * hidden_ref[...].astype(jnp.float32)
        ).astype(jnp.bfloat16)

    return body


def finish(step, holder):
    def body(time_ref, size_ref, got_ref, out_ref):
        for micro in range(out_ref.shape[0]):
            size = size_ref[time_ref[step, micro]]
            slot = got_ref[0, micro].astype(jnp.float32)
            hidden = got_ref[holder, micro].astype(jnp.float32)
            out_ref[micro] = (slot - size * hidden).astype(jnp.bfloat16)

    return body


def shards(latents, timesteps, step_sizes, mod_table, qk_gain, w_query, w_kv, w_out):
    n_pipe = lax.axis_size("pipe")
    n_seq = lax.axis_size("seq")
    pipe_at = lax.axis_index("pipe")
    seq_at = lax.axis_index("seq")
    core = seq_at % 2
    micro = (seq_at // 2) % 2
    micro_count, row_share, feature_share = latents.shape
    step_count = timesteps.shape[0]
    tokens = row_share * n_seq
    width = feature_share * n_pipe
    half = width // 2
    head_dim = qk_gain.shape[2]
    core_pairs = [(at, at ^ 1) for at in range(n_seq)]
    quads = [[4 * at + j for j in range(4)] for at in range(n_seq // 4)]

    def swapped(value):
        return lax.ppermute(value, "seq", core_pairs)

    def columns(value, side, axis):
        return lax.dynamic_slice_in_dim(value, side * half, half, axis)

    def kv_columns(side):
        keys, values = w_kv[0, :, :width], w_kv[0, :, width:]
        return jnp.concatenate([columns(keys, side, 1), columns(values, side, 1)], axis=1)

    mine = kv_columns(core)
    theirs = swapped(kv_columns(1 - core))
    low = jnp.where(core == 0, mine, theirs)
    high = jnp.where(core == 0, theirs, mine)
    block = jnp.concatenate([low, high], axis=0)
    latents, block = lax.optimization_barrier((latents, block))
    theirs = lax.ppermute(block, "seq", [(at, at ^ 2) for at in range(n_seq)])

    sent = jnp.broadcast_to(latents[None], (n_pipe,) + latents.shape)
    rows = lax.all_to_all(sent, "pipe", 0, 0, tiled=True)
    low = jnp.where(micro == 0, block, theirs)
    high = jnp.where(micro == 0, theirs, block)
    block = jnp.concatenate([low, high], axis=0)
    backward = [(at + 1, at) for at in range(0, n_pipe, 2)]

    def to_even(value):
        return lax.ppermute(value, "pipe", backward)

    rows, block = lax.optimization_barrier((rows, block))
    ring = n_seq // 4
    rings = [[(at, (at + turn) % n_seq) for at in range(n_seq)] for turn in (4, -4)]
    middle = block.shape[0] // 2
    rising = falling = block
    parts = [block]
    spots = [(0, 0)]
    for turn in range(1, ring // 2):
        rising = lax.ppermute(rising, "seq", rings[0])
        falling = lax.ppermute(falling, "seq", rings[1])
        parts += [rising, falling]
        spots += [(ring - turn, 0), (turn, 0)]
        if turn == 1:
            rows, rising, falling = lax.optimization_barrier((rows, rising, falling))
    parts += [
        lax.ppermute(rising[:middle], "seq", rings[0]),
        lax.ppermute(falling[middle:], "seq", rings[1]),
    ]
    spots += [(ring // 2, 0), (ring // 2, middle)]

    rows = jnp.transpose(rows, (1, 2, 0, 3)).reshape(micro_count, row_share, 2, half)
    sent = jnp.transpose(rows, (0, 2, 1, 3)).reshape(1, 4, row_share, half)
    sent = jnp.broadcast_to(sent, (n_seq // 4, 4, row_share, half)).reshape(
        n_seq, row_share, half
    )
    slot = lax.all_to_all(sent, "seq", 0, 0, tiled=True).reshape(tokens, half)

    next_table, next_gain = to_even(mod_table), to_even(qk_gain)
    parts[-1], next_table, next_gain = lax.optimization_barrier(
        (parts[-1], next_table, next_gain)
    )
    words = jnp.stack([core, micro, seq_at // 4]).astype(jnp.int32)
    smem = pl.BlockSpec(memory_space=pltpu.SMEM)
    vmem = pl.BlockSpec(memory_space=pltpu.VMEM)
    hbm = pl.BlockSpec(memory_space=pltpu.HBM)
    held_shape = jax.ShapeDtypeStruct((width, 2 * width), jnp.bfloat16)
    small_shapes = [jax.ShapeDtypeStruct(qk_gain.shape[1:], jnp.float32)] * 2 + [
        jax.ShapeDtypeStruct((6, half), jnp.float32)
    ] * (1 + step_count)

    def in_hbm(value):
        return pltpu.with_memory_space_constraint(value, pltpu.HBM)

    loaded = pl.pallas_call(
        load_own(spots),
        out_shape=[held_shape] + small_shapes,
        in_specs=[smem] + [hbm] * len(parts) + [smem] + [vmem] * 4 + [hbm, hbm],
        out_specs=[vmem] * (4 + step_count),
        scratch_shapes=[pltpu.SemaphoreType.DMA((len(parts) + 4,))],
        compiler_params=pltpu.CompilerParams(vmem_limit_bytes=12 << 20),
        name="load_own",
    )(
        words,
        *(in_hbm(part) for part in parts),
        timesteps,
        mod_table,
        qk_gain,
        next_table,
        next_gain,
        in_hbm(w_query),
        in_hbm(w_out),
    )
    held, gains, next_gains, next_mods = loaded[:4]
    mods = loaded[4:]

    def layer(hidden, mods, gains, weights):
        attended = pl.pallas_call(
            layer_front(head_dim),
            out_shape=jax.ShapeDtypeStruct((tokens, half), jnp.bfloat16),
            in_specs=[vmem] * 5,
            out_specs=vmem,
            compiler_params=pltpu.CompilerParams(vmem_limit_bytes=16 << 20),
            name="front",
        )(hidden, swapped(hidden), mods, gains, weights)
        return pl.pallas_call(
            layer_back,
            out_shape=jax.ShapeDtypeStruct((tokens, half), jnp.bfloat16),
            in_specs=[vmem] * 5,
            out_specs=vmem,
            compiler_params=pltpu.CompilerParams(vmem_limit_bytes=12 << 20),
            name="back",
        )(attended, swapped(attended), hidden, mods, weights)

    apart = 2
    held_pairs = [(at + 1, at) for at in range(apart, n_pipe, 2)]
    following = [next_mods, next_gains, lax.ppermute(held, "pipe", held_pairs)]

    holder = 0
    hidden = slot
    for step in range(step_count):
        for section in range(n_pipe):
            joined = step > 0 and section >= apart
            place = section - section % 2 if joined else section
            if place != holder:
                hidden = lax.ppermute(hidden, "pipe", [(holder, place)])
                holder = place
            if step > 0 and section == 2:
                hidden, following[2] = lax.optimization_barrier((hidden, following[2]))
            if step > 0 and section == 0:
                slot = pl.pallas_call(
                    advance_slot(step - 1),
                    out_shape=jax.ShapeDtypeStruct((tokens, half), jnp.bfloat16),
                    in_specs=[smem] * 3 + [vmem] * 2,
                    out_specs=vmem,
                    compiler_params=pltpu.CompilerParams(vmem_limit_bytes=8 << 20),
                    name="advance_slot",
                )(words, timesteps, step_sizes, slot, hidden)
                hidden = slot
            hidden = layer(hidden, *(following if section != place else (mods[step], gains, held)))

    kept = jnp.where(pipe_at == 0, slot, hidden)
    kept = lax.dynamic_slice_in_dim(kept, (seq_at // 4) * 4 * row_share, 4 * row_share, 0)
    kept = kept.reshape(4, row_share, half)
    kept = lax.all_to_all(kept, "seq", 0, 0, tiled=True, axis_index_groups=quads)
    kept = kept.reshape(micro_count, 2, row_share, n_pipe // 2, feature_share)
    sent = jnp.transpose(kept, (1, 3, 0, 2, 4)).reshape(
        n_pipe, micro_count, row_share, feature_share
    )
    got = lax.all_to_all(sent, "pipe", 0, 0, tiled=True)
    return pl.pallas_call(
        finish(step_count - 1, holder),
        out_shape=jax.ShapeDtypeStruct(latents.shape, jnp.bfloat16),
        in_specs=[smem] * 2 + [vmem],
        out_specs=vmem,
        compiler_params=pltpu.CompilerParams(vmem_limit_bytes=8 << 20),
        name="finish",
    )(timesteps, step_sizes, got)


def solution(mesh):
    in_specs = (
        P(None, "seq", "pipe"),
        P(),
        P(),
        P("pipe", None, None),
        P("pipe", None, None),
        P("pipe", None, None),
        P("pipe", "seq", None),
        P("pipe", None, None),
    )
    out_specs = P(None, "seq", "pipe")
    return jax.shard_map(shards, mesh=mesh, in_specs=in_specs, out_specs=out_specs, check_vma=False)
```

```python
import math

import jax
import jax.numpy as jnp
from jax import lax
from jax.experimental import pallas as pl
from jax.experimental.pallas import tpu as pltpu
from jax.sharding import PartitionSpec as P

norm_eps = 1e-06


def layer_front(head_dim):
    score_scale = 1.0 / math.sqrt(head_dim)

    def body(own_ref, other_ref, mod_ref, gain_ref, weight_ref, out_ref):
        half = own_ref.shape[1]
        width = 2 * half
        own = own_ref[...].astype(jnp.float32)
        other = other_ref[...].astype(jnp.float32)
        center = (
            jnp.sum(own, axis=-1, keepdims=True) + jnp.sum(other, axis=-1, keepdims=True)
        ) / width
        own = own - center
        other = other - center
        spread = (
            jnp.sum(own * own, axis=-1, keepdims=True)
            + jnp.sum(other * other, axis=-1, keepdims=True)
        ) / width
        inverse = lax.rsqrt(spread + norm_eps)

        def modulated(values, at):
            shift_row = mod_ref[at : at + 1, :]
            scale_row = mod_ref[2 + at : 3 + at, :]
            return (values * inverse * (1.0 + scale_row) + shift_row).astype(jnp.bfloat16)

        own = modulated(own, 0)
        other = modulated(other, 1)

        def project(start, size):
            cols = slice(start, start + size)
            return jnp.dot(
                own, weight_ref[:half, cols], preferred_element_type=jnp.float32
            ) + jnp.dot(other, weight_ref[half:, cols], preferred_element_type=jnp.float32)

        def rms(values, gain_row):
            mean_square = jnp.mean(values * values, axis=-1, keepdims=True)
            return (values * lax.rsqrt(mean_square + norm_eps) * gain_row).astype(jnp.bfloat16)

        gain_query = gain_ref[0:1, :]
        gain_key = gain_ref[1:2, :]
        group = 2 * head_dim
        for start in range(0, half, group):
            queries = project(start, group)
            keys = project(half + start, group)
            values = project(2 * half + start, group).astype(jnp.bfloat16)
            for at in range(0, group, head_dim):
                query_head = rms(queries[:, at : at + head_dim], gain_query)
                key_head = rms(keys[:, at : at + head_dim], gain_key)
                logits = (
                    lax.dot_general(
                        query_head,
                        key_head,
                        (((1,), (1,)), ((), ())),
                        preferred_element_type=jnp.float32,
                    )
                    * score_scale
                )
                weights = jnp.exp(logits)
                total = jnp.sum(weights, axis=-1, keepdims=True)
                mixed = jnp.dot(
                    weights.astype(jnp.bfloat16),
                    values[:, at : at + head_dim],
                    preferred_element_type=jnp.float32,
                )
                out_ref[:, start + at : start + at + head_dim] = (mixed / total).astype(
                    jnp.bfloat16
                )

    return body


def layer_back(own_ref, other_ref, hidden_ref, mod_ref, weight_ref, out_ref):
    half = own_ref.shape[1]
    cols = slice(3 * half, 4 * half)
    projected = jnp.dot(
        own_ref[...], weight_ref[:half, cols], preferred_element_type=jnp.float32
    ) + jnp.dot(other_ref[...], weight_ref[half:, cols], preferred_element_type=jnp.float32)
    out_ref[...] = (
        hidden_ref[...].astype(jnp.float32) + mod_ref[4:5, :] * projected
    ).astype(jnp.bfloat16)


def load_own(spots):
    def body(word_ref, *refs):
        part_refs = refs[: len(spots)]
        time_ref, mod_ref, gain_ref, next_mod_ref, next_gain_ref, query_ref, out_ref = refs[
            len(spots) : len(spots) + 7
        ]
        held_ref, gain_held, next_gain_held, next_mods_held = refs[
            len(spots) + 7 : len(spots) + 11
        ]
        mods_held, sems = refs[len(spots) + 11 : -1], refs[-1]
        core = word_ref[0]
        width = held_ref.shape[0]
        half = width // 2
        block = part_refs[0].shape[0]
        ring = width // block
        copies = []

        def copied(source, target):
            copies.append(pltpu.make_async_copy(source, target, sems.at[len(copies)]))

        for (turn, start), part_ref in zip(spots, part_refs):
            rows = part_ref.shape[0]
            at = lax.rem(word_ref[2] + turn + core * (ring // 2), ring) * block + start
            copied(
                part_ref, held_ref.at[pl.ds(pl.multiple_of(at, rows), rows), pl.ds(half, width)]
            )
        cols = pl.ds(pl.multiple_of(core * half, half), half)
        for source, left in ((query_ref, 0), (out_ref, half + width)):
            for side in range(2):
                first = pl.multiple_of(lax.rem(core + side, 2) * half, half)
                copied(
                    source.at[0, pl.ds(first, half), cols],
                    held_ref.at[pl.ds(side * half, half), pl.ds(left, half)],
                )
        for copy in copies:
            copy.start()
        gain_held[...] = gain_ref[0]
        next_gain_held[...] = next_gain_ref[0]

        def picked(table_ref, step, held):
            row = pl.ds(time_ref[step, word_ref[1]], 1)
            for third in range(3):
                for side in range(2):
                    first = (2 * third + lax.rem(core + side, 2)) * half
                    first = pl.ds(pl.multiple_of(first, half), half)
                    held[2 * third + side : 2 * third + side + 1, :] = table_ref[0, row, first]

        for step, held in enumerate(mods_held):
            picked(mod_ref, step, held)
        picked(next_mod_ref, len(mods_held) - 1, next_mods_held)
        for copy in copies:
            copy.wait()

    return body


def advance_slot(step):
    def body(word_ref, time_ref, size_ref, slot_ref, hidden_ref, out_ref):
        size = size_ref[time_ref[step, word_ref[1]]]
        out_ref[...] = (
            slot_ref[...].astype(jnp.float32) - size * hidden_ref[...].astype(jnp.float32)
        ).astype(jnp.bfloat16)

    return body


def finish(step, holder):
    def body(time_ref, size_ref, got_ref, out_ref):
        for micro in range(out_ref.shape[0]):
            size = size_ref[time_ref[step, micro]]
            slot = got_ref[0, micro].astype(jnp.float32)
            hidden = got_ref[holder, micro].astype(jnp.float32)
            out_ref[micro] = (slot - size * hidden).astype(jnp.bfloat16)

    return body


def shards(latents, timesteps, step_sizes, mod_table, qk_gain, w_query, w_kv, w_out):
    n_pipe = lax.axis_size("pipe")
    n_seq = lax.axis_size("seq")
    pipe_at = lax.axis_index("pipe")
    seq_at = lax.axis_index("seq")
    core = seq_at % 2
    micro = (seq_at // 2) % 2
    micro_count, row_share, feature_share = latents.shape
    step_count = timesteps.shape[0]
    tokens = row_share * n_seq
    width = feature_share * n_pipe
    half = width // 2
    head_dim = qk_gain.shape[2]
    core_pairs = [(at, at ^ 1) for at in range(n_seq)]
    quads = [[4 * at + j for j in range(4)] for at in range(n_seq // 4)]

    def swapped(value):
        return lax.ppermute(value, "seq", core_pairs)

    def columns(value, side, axis):
        return lax.dynamic_slice_in_dim(value, side * half, half, axis)

    def kv_columns(side):
        keys, values = w_kv[0, :, :width], w_kv[0, :, width:]
        return jnp.concatenate([columns(keys, side, 1), columns(values, side, 1)], axis=1)

    mine = kv_columns(core)
    theirs = swapped(kv_columns(1 - core))
    low = jnp.where(core == 0, mine, theirs)
    high = jnp.where(core == 0, theirs, mine)
    block = jnp.concatenate([low, high], axis=0)
    latents, block = lax.optimization_barrier((latents, block))
    theirs = lax.ppermute(block, "seq", [(at, at ^ 2) for at in range(n_seq)])

    sent = jnp.broadcast_to(latents[None], (n_pipe,) + latents.shape)
    rows = lax.all_to_all(sent, "pipe", 0, 0, tiled=True)
    low = jnp.where(micro == 0, block, theirs)
    high = jnp.where(micro == 0, theirs, block)
    block = jnp.concatenate([low, high], axis=0)
    backward = [(at + 1, at) for at in range(0, n_pipe, 2)]

    def to_even(value):
        return lax.ppermute(value, "pipe", backward)

    rows, block = lax.optimization_barrier((rows, block))
    ring = n_seq // 4
    rings = [[(at, (at + turn) % n_seq) for at in range(n_seq)] for turn in (4, -4)]
    middle = block.shape[0] // 2
    rising = falling = block
    parts = [block]
    spots = [(0, 0)]
    for turn in range(1, ring // 2):
        rising = lax.ppermute(rising, "seq", rings[0])
        falling = lax.ppermute(falling, "seq", rings[1])
        parts += [rising, falling]
        spots += [(ring - turn, 0), (turn, 0)]
        if turn == 1:
            rows, rising, falling = lax.optimization_barrier((rows, rising, falling))
    parts += [
        lax.ppermute(rising[:middle], "seq", rings[0]),
        lax.ppermute(falling[middle:], "seq", rings[1]),
    ]
    spots += [(ring // 2, 0), (ring // 2, middle)]

    rows = jnp.transpose(rows, (1, 2, 0, 3)).reshape(micro_count, row_share, 2, half)
    sent = jnp.transpose(rows, (0, 2, 1, 3)).reshape(1, 4, row_share, half)
    sent = jnp.broadcast_to(sent, (n_seq // 4, 4, row_share, half)).reshape(
        n_seq, row_share, half
    )
    slot = lax.all_to_all(sent, "seq", 0, 0, tiled=True).reshape(tokens, half)

    next_table, next_gain = to_even(mod_table), to_even(qk_gain)
    parts[-1], next_table, next_gain = lax.optimization_barrier(
        (parts[-1], next_table, next_gain)
    )
    words = jnp.stack([core, micro, seq_at // 4]).astype(jnp.int32)
    smem = pl.BlockSpec(memory_space=pltpu.SMEM)
    vmem = pl.BlockSpec(memory_space=pltpu.VMEM)
    hbm = pl.BlockSpec(memory_space=pltpu.HBM)
    held_shape = jax.ShapeDtypeStruct((width, 2 * width), jnp.bfloat16)
    small_shapes = [jax.ShapeDtypeStruct(qk_gain.shape[1:], jnp.float32)] * 2 + [
        jax.ShapeDtypeStruct((6, half), jnp.float32)
    ] * (1 + step_count)

    def in_hbm(value):
        return pltpu.with_memory_space_constraint(value, pltpu.HBM)

    loaded = pl.pallas_call(
        load_own(spots),
        out_shape=[held_shape] + small_shapes,
        in_specs=[smem] + [hbm] * len(parts) + [smem] + [vmem] * 4 + [hbm, hbm],
        out_specs=[vmem] * (4 + step_count),
        scratch_shapes=[pltpu.SemaphoreType.DMA((len(parts) + 4,))],
        compiler_params=pltpu.CompilerParams(vmem_limit_bytes=12 << 20),
        name="load_own",
    )(
        words,
        *(in_hbm(part) for part in parts),
        timesteps,
        mod_table,
        qk_gain,
        next_table,
        next_gain,
        in_hbm(w_query),
        in_hbm(w_out),
    )
    held, gains, next_gains, next_mods = loaded[:4]
    mods = loaded[4:]

    def layer(hidden, mods, gains, weights):
        attended = pl.pallas_call(
            layer_front(head_dim),
            out_shape=jax.ShapeDtypeStruct((tokens, half), jnp.bfloat16),
            in_specs=[vmem] * 5,
            out_specs=vmem,
            compiler_params=pltpu.CompilerParams(vmem_limit_bytes=16 << 20),
            name="front",
        )(hidden, swapped(hidden), mods, gains, weights)
        return pl.pallas_call(
            layer_back,
            out_shape=jax.ShapeDtypeStruct((tokens, half), jnp.bfloat16),
            in_specs=[vmem] * 5,
            out_specs=vmem,
            compiler_params=pltpu.CompilerParams(vmem_limit_bytes=12 << 20),
            name="back",
        )(attended, swapped(attended), hidden, mods, weights)

    apart = 4
    held_pairs = [(at + 1, at) for at in range(apart, n_pipe, 2)]
    following = [next_mods, next_gains, lax.ppermute(held, "pipe", held_pairs)]

    holder = 0
    hidden = slot
    for step in range(step_count):
        for section in range(n_pipe):
            joined = step > 0 and section >= apart
            place = section - section % 2 if joined else section
            if place != holder:
                hidden = lax.ppermute(hidden, "pipe", [(holder, place)])
                holder = place
            if step > 0 and section == 0:
                hidden, following[2] = lax.optimization_barrier((hidden, following[2]))
                slot = pl.pallas_call(
                    advance_slot(step - 1),
                    out_shape=jax.ShapeDtypeStruct((tokens, half), jnp.bfloat16),
                    in_specs=[smem] * 3 + [vmem] * 2,
                    out_specs=vmem,
                    compiler_params=pltpu.CompilerParams(vmem_limit_bytes=8 << 20),
                    name="advance_slot",
                )(words, timesteps, step_sizes, slot, hidden)
                hidden = slot
            hidden = layer(hidden, *(following if section != place else (mods[step], gains, held)))

    kept = jnp.where(pipe_at == 0, slot, hidden)
    kept = lax.dynamic_slice_in_dim(kept, (seq_at // 4) * 4 * row_share, 4 * row_share, 0)
    kept = kept.reshape(4, row_share, half)
    kept = lax.all_to_all(kept, "seq", 0, 0, tiled=True, axis_index_groups=quads)
    kept = kept.reshape(micro_count, 2, row_share, n_pipe // 2, feature_share)
    sent = jnp.transpose(kept, (1, 3, 0, 2, 4)).reshape(
        n_pipe, micro_count, row_share, feature_share
    )
    got = lax.all_to_all(sent, "pipe", 0, 0, tiled=True)
    return pl.pallas_call(
        finish(step_count - 1, holder),
        out_shape=jax.ShapeDtypeStruct(latents.shape, jnp.bfloat16),
        in_specs=[smem] * 2 + [vmem],
        out_specs=vmem,
        compiler_params=pltpu.CompilerParams(vmem_limit_bytes=8 << 20),
        name="finish",
    )(timesteps, step_sizes, got)


def solution(mesh):
    in_specs = (
        P(None, "seq", "pipe"),
        P(),
        P(),
        P("pipe", None, None),
        P("pipe", None, None),
        P("pipe", None, None),
        P("pipe", "seq", None),
        P("pipe", None, None),
    )
    out_specs = P(None, "seq", "pipe")
    return jax.shard_map(shards, mesh=mesh, in_specs=in_specs, out_specs=out_specs, check_vma=False)
```
